128 devices in a mesh: depth: 2 (over core), tiles: 64 (over z, y, x).
Axes of the slice: x: 4, y: 4, z: 4, core: 2. Of those that a mesh axis runs over, the one named last changes fastest.
Arguments:
- transmission: float32 [4, 2, 64, 256, 256], P('depth', None, 'tiles'), may hold values from -0.4 to 1.3
- illumination: float32 [2, 256, 256], replicated, may hold values from -6 to 6
- fresnel_taps: float32 [2, 31], replicated, may hold values from -1 to 1
- intensity: float32 [64, 2, 256, 256], P('tiles'), may hold values from 0 to 2
- offsets: int32 [64, 2, 2], P('tiles'), may hold values from 0 to 255, as said below
- counts: int32 [64], P('tiles'), may hold values from 0 to 2, as said below
Outputs:
- object_gradient: float32 [4, 2, 64, 256, 256], P('depth', None, 'tiles')
The draws below stay inside these ranges and needn't reach their ends.
Inputs may be any that keep to these rules, and one draw needn't show every extreme that they name: `offsets`: A tile in the last row of tiles has row offset 0 in every slot, and a tile in the last column of tiles has column offset 0 in every slot, so every patch lies inside the object. Slots j >= counts[t] of tile t are unused.
All inputs are finite; a program needn't handle non-finite values.
Results may differ from the reference program's by a relative error of at most 0.0003.
Values sent between devices are 32-bit elements; how exact they have to be, the bound alone decides.
No kernel may reach another device: no remote copies, remote signals or barrier semaphores. Data moves between devices by JAX's collectives and lax.ppermute only.
A program may use at most 64 MiB of HBM per device.

```python
import math
import jax
import jax.numpy as jnp
from jax import lax

P_SIZE = 256
KT = 31
GX = 4
CAP = 2
S = 256
SLICES = 4
TILE_COUNT = 64


sample_total = 64


def draw_transmission(key, part):
    key_real = jax.random.fold_in(key, 11)
    key_imag = jax.random.fold_in(key, 12)
    shape_one = (SLICES, TILE_COUNT, S, S)
    real_part = jax.random.uniform(key_real, shape_one, jnp.float32, 0.65, 1.25)
    imag_part = jax.random.uniform(key_imag, shape_one, jnp.float32, -0.3, 0.3)
    return jnp.stack([real_part, imag_part], 1)


def draw_fresnel_taps(key, part):
    key_main = jax.random.fold_in(key, 41)
    key_fourth = jax.random.fold_in(key, 42)
    key_tilt = jax.random.fold_in(key, 43)
    strength = jax.random.uniform(key_main, (), jnp.float32, 2.0, 4.0)
    fourth = jax.random.uniform(key_fourth, (), jnp.float32, -0.5, 0.5)
    tilt = jax.random.uniform(key_tilt, (), jnp.float32, -0.5, 0.5)
    half_taps = KT // 2
    lag_values = (lax.broadcasted_iota(jnp.int32, (KT, sample_total), 0) - half_taps).astype(jnp.float32)
    theta = lax.broadcasted_iota(jnp.int32, (KT, sample_total), 1).astype(jnp.float32) * (2.0 * math.pi / sample_total)
    phase = strength * jnp.cos(theta) + fourth * jnp.cos(2.0 * theta) + tilt * jnp.sin(theta) + lag_values * theta
    taps_real = jnp.mean(jnp.cos(phase), axis=1)
    taps_imag = jnp.mean(jnp.sin(phase), axis=1)
    return jnp.stack([taps_real, taps_imag], 0)


def draw_offsets(key, part):
    key_row = jax.random.fold_in(key, 21)
    key_col = jax.random.fold_in(key, 22)
    tile_index = lax.broadcasted_iota(jnp.int32, (TILE_COUNT, CAP), 0)
    slot_index = lax.broadcasted_iota(jnp.int32, (TILE_COUNT, CAP), 1)
    row_offset = jax.random.randint(key_row, (TILE_COUNT, CAP), 0, S, dtype=jnp.int32)
    col_offset = jax.random.randint(key_col, (TILE_COUNT, CAP), 0, S, dtype=jnp.int32)
    first_slot = (tile_index == 0) & (slot_index == 0)
    row_offset = jnp.where(first_slot, S - 1, row_offset)
    col_offset = jnp.where(first_slot, S - 1, col_offset)
    row_offset = jnp.where(tile_index // GX < TILE_COUNT // GX - 1, row_offset, 0)
    col_offset = jnp.where(tile_index % GX < GX - 1, col_offset, 0)
    return jnp.stack([row_offset, col_offset], -1)


def draw_counts(key, part):
    key_base = jax.random.fold_in(key, 31)
    key_busy = jax.random.fold_in(key, 32)
    tile_index = lax.broadcasted_iota(jnp.int32, (TILE_COUNT,), 0)
    base_counts = jax.random.randint(key_base, (TILE_COUNT,), 0, CAP + 1, dtype=jnp.int32)
    busiest = jax.random.randint(key_busy, (), 0, TILE_COUNT, dtype=jnp.int32)
    emptiest = (busiest + 1) % TILE_COUNT
    base_counts = jnp.where(tile_index == busiest, CAP, base_counts)
    return jnp.where(tile_index == emptiest, 0, base_counts)


def level_of(stream_key, dims, cuts, low, largest):
    def one(dim, shards_of):
        heights = jax.random.uniform(jax.random.fold_in(jax.random.fold_in(stream_key, 6), dim), (shards_of,), jnp.float32, low / len(cuts), largest / len(cuts))
        return jnp.repeat(jnp.exp(heights), dims[dim] // shards_of).reshape((-1,) + (1,) * (len(dims) - dim - 1))

    gain = one(*cuts[0])
    for cut in cuts[1:]:
        gain = gain * one(*cut)
    return gain


def centred(key, dims, scale, bound, kind=jnp.bfloat16):
    return jnp.clip(scale * jax.random.normal(key, dims, jnp.float32), -bound, bound).astype(kind)


def setup_inputs(seed: int = 0) -> dict:
    keys = jax.random.split(jax.random.key(seed), 7)
    transmission = draw_transmission(jax.random.fold_in(keys[6], 71), 0)
    illumination = centred(keys[1], (2, P_SIZE, P_SIZE), 1.0, 6.0, jnp.float32)
    fresnel_taps = draw_fresnel_taps(jax.random.fold_in(keys[6], 71), 0)
    intensity = jnp.clip(2.0 * jax.random.uniform(keys[3], (TILE_COUNT, CAP, P_SIZE, P_SIZE), jnp.float32) ** level_of(keys[3], (TILE_COUNT, CAP, P_SIZE, P_SIZE), ((0, 64),), -0.2, 0.2), 0.0, 2.0)
    offsets = draw_offsets(jax.random.fold_in(keys[6], 71), 0)
    counts = draw_counts(jax.random.fold_in(keys[6], 71), 0)
    return dict(transmission=transmission, illumination=illumination, fresnel_taps=fresnel_taps, intensity=intensity, offsets=offsets, counts=counts)


def convolve(field_real, field_imag, fresnel_taps, axis_no):
    half_taps = fresnel_taps.shape[1] // 2
    extent = field_real.shape[axis_no]
    padding = [(0, 0), (0, 0)]
    padding[axis_no] = (half_taps, half_taps)
    padded_real = jnp.pad(field_real, padding)
    padded_imag = jnp.pad(field_imag, padding)
    result_real = jnp.zeros_like(field_real)
    result_imag = jnp.zeros_like(field_imag)
    for tap_index in range(fresnel_taps.shape[1]):
        moved_real = lax.slice_in_dim(padded_real, tap_index, tap_index + extent, axis=axis_no)
        moved_imag = lax.slice_in_dim(padded_imag, tap_index, tap_index + extent, axis=axis_no)
        tap_real = fresnel_taps[0, tap_index]
        tap_imag = fresnel_taps[1, tap_index]
        result_real = result_real + tap_real * moved_real - tap_imag * moved_imag
        result_imag = result_imag + tap_imag * moved_real + tap_real * moved_imag
    return (result_real, result_imag)

def patch_misfit(patches, illumination, fresnel_taps, measured, live_flag):
    wave_real = illumination[0]
    wave_imag = illumination[1]
    for slice_index in range(SLICES):
        object_real = patches[slice_index, 0]
        object_imag = patches[slice_index, 1]
        mixed_real = wave_real * object_real - wave_imag * object_imag
        mixed_imag = wave_real * object_imag + wave_imag * object_real
        half_real, half_imag = convolve(mixed_real, mixed_imag, fresnel_taps, 0)
        wave_real, wave_imag = convolve(half_real, half_imag, fresnel_taps, 1)
    spectrum = jnp.fft.fft2(wave_real + 1j * wave_imag, norm='ortho')
    power = jnp.real(spectrum) ** 2 + jnp.imag(spectrum) ** 2
    misfit = live_flag * (power - measured)
    return 0.5 * jnp.sum(misfit * misfit)

def assemble(tiled):
    tile_rows = TILE_COUNT // GX
    shaped = tiled.reshape(SLICES, 2, tile_rows, GX, S, S)
    shaped = jnp.transpose(shaped, (0, 1, 2, 4, 3, 5))
    return shaped.reshape(SLICES, 2, tile_rows * S, GX * S)

def disassemble(whole):
    tile_rows = TILE_COUNT // GX
    shaped = whole.reshape(SLICES, 2, tile_rows, S, GX, S)
    shaped = jnp.transpose(shaped, (0, 1, 2, 4, 3, 5))
    return shaped.reshape(SLICES, 2, TILE_COUNT, S, S)

def reference(transmission, illumination, fresnel_taps, intensity, offsets, counts):
    whole = assemble(transmission)
    flat_offsets = offsets.reshape(TILE_COUNT * CAP, 2).astype(jnp.int32)
    tile_ids = jnp.repeat(jnp.arange(TILE_COUNT, dtype=jnp.int32), CAP)
    slot_ids = jnp.tile(jnp.arange(CAP, dtype=jnp.int32), TILE_COUNT)
    live_all = (slot_ids < counts[tile_ids]).astype(whole.dtype)
    measured_all = intensity.reshape(TILE_COUNT * CAP, P_SIZE, P_SIZE)
    row_starts = (tile_ids // GX * S + flat_offsets[:, 0]).astype(jnp.int32)
    col_starts = (tile_ids % GX * S + flat_offsets[:, 1]).astype(jnp.int32)
    zero_index = jnp.zeros((), jnp.int32)

    def accumulate(gradient, item):
        row_start, col_start, measured, live_flag = item
        corner = (zero_index, zero_index, row_start, col_start)
        patches = lax.dynamic_slice(whole, corner, (SLICES, 2, P_SIZE, P_SIZE))
        loss, pullback = jax.vjp(lambda block: patch_misfit(block, illumination, fresnel_taps, measured, live_flag), patches)
        patch_gradient, = pullback(jnp.ones_like(loss))
        current = lax.dynamic_slice(gradient, corner, (SLICES, 2, P_SIZE, P_SIZE))
        return (lax.dynamic_update_slice(gradient, current + patch_gradient, corner), None)
    gradient, unused = lax.scan(accumulate, jnp.zeros_like(whole), (row_starts, col_starts, measured_all, live_all))
    return disassemble(gradient)
```

```python
import functools
import math

import jax
import jax.numpy as jnp
from jax import lax
from jax.experimental import pallas as pl
from jax.experimental.pallas import tpu as pltpu
from jax.sharding import PartitionSpec as P

GX = 4
ROWS = 16
TILES = 64
N = 256
CH = 32
BF = jnp.bfloat16
F32 = jnp.float32
FIELD = jax.ShapeDtypeStruct((2, N, N), F32)
VS = pl.BlockSpec(memory_space=pltpu.VMEM)
SS = pl.BlockSpec(memory_space=pltpu.SMEM)


def split(x):
    high = x.astype(BF)
    return high, (x - high.astype(F32)).astype(BF)


def dot3(left_high, left_low, right_high, right_low):
    dot = functools.partial(jnp.dot, preferred_element_type=F32)
    return dot(left_high, right_high) + dot(left_high, right_low) + dot(left_low, right_high)


def put_left(refs, index, re, im):
    for ref, r, m in zip(refs, split(re), split(im)):
        ref[index, 0:N, 0:N] = r
        ref[index, N : 2 * N, N : 2 * N] = r
        ref[index, N : 2 * N, 0:N] = m
        ref[index, 0:N, N : 2 * N] = -m


def put_right(refs, index, re, im):
    for ref, r, m in zip(refs, split(re), split(im)):
        ref[index, 0:N] = r
        ref[index, N : 2 * N] = m


def tables_kernel(spot, taps, dft, left_high, left_low, right_high, right_low, a_high, a_low, b_high, b_low):
    left = (left_high, left_low)
    right = (right_high, right_low)
    a = (a_high, a_low)
    b = (b_high, b_low)
    row = lax.broadcasted_iota(jnp.int32, (N, N), 0)
    col = lax.broadcasted_iota(jnp.int32, (N, N), 1)

    def circulant(k):
        base = jnp.broadcast_to(taps[k : k + 1, :], (N, N))
        return pltpu.roll(base, 0, 1, stride=1, stride_axis=0)

    rings = [circulant(k) for k in range(4)]
    fr, fi = dft[0], dft[1]

    def bands(shift):
        inside = jnp.abs(((row - shift) & (N - 1)) - ((col - shift) & (N - 1))) <= 15
        return [jnp.where(inside, ring, 0.0) for ring in rings]

    def multiply():
        m = dot3(a_high[0], a_low[0], b_high[0], b_low[0])
        return m[:N], m[N:]

    tr, ti, ttr, tti = bands(spot[0])
    put_left(left, 0, tr, ti)
    put_left(left, 1, ttr, -tti)
    put_left(a, 0, fr, fi)
    put_right(b, 0, tr, ti)
    mr, mi = multiply()
    put_left(left, 2, mr, mi)
    put_left(a, 0, ttr, tti)
    put_right(b, 0, fr, fi)
    mr, mi = multiply()
    put_left(left, 3, mr, -mi)
    tr, ti, ttr, tti = bands(spot[1])
    put_right(right, 0, ttr, tti)
    put_right(right, 1, tr, -ti)
    put_left(a, 0, ttr, tti)
    mr, mi = multiply()
    put_right(right, 2, mr, mi)
    put_left(a, 0, fr, fi)
    put_right(b, 0, tr, ti)
    mr, mi = multiply()
    put_right(right, 3, mr, -mi)


def tables(spot, taps, dft):
    return pl.pallas_call(
        tables_kernel,
        out_shape=[jax.ShapeDtypeStruct((4, 2 * N, 2 * N), BF)] * 2
        + [jax.ShapeDtypeStruct((4, 2 * N, N), BF)] * 2,
        in_specs=[SS, VS, VS],
        out_specs=[VS] * 4,
        scratch_shapes=[pltpu.VMEM((1, 2 * N, 2 * N), BF)] * 2 + [pltpu.VMEM((1, 2 * N, N), BF)] * 2,
        compiler_params=pltpu.CompilerParams(vmem_limit_bytes=12 << 20),
        name="tables",
    )(spot, taps, dft)


def tap_rows(taps):
    rows = jnp.concatenate([taps, taps[:, ::-1]], 0)
    rows = jnp.pad(rows, ((0, 4), (0, N - rows.shape[1])))
    return jnp.roll(rows, -15, 1)


def chunks():
    return [(pl.ds(r0, CH), pl.ds(N + r0, CH), r0) for r0 in range(0, N, CH)]


def own_rows(spot, r0):
    row = lax.broadcasted_iota(jnp.int32, (CH, N), 0) + r0
    return ((row >= spot[0]).astype(jnp.int32) ^ spot[2]) == 1


def own_cols(spot):
    col = lax.broadcasted_iota(jnp.int32, (CH, N), 1)
    return ((col >= spot[1]).astype(jnp.int32) ^ spot[2]) == 1


WORK = (
    [pltpu.VMEM((2 * N, N), BF)] * 2
    + [pltpu.VMEM((2 * N, 2 * N), BF)] * 2
    + [pltpu.VMEM((2 * N, N), F32)]
)


def put_field(work, r0, re, im):
    for base, part in ((0, re), (N, im)):
        high, low = split(part)
        work[0][pl.ds(base + r0, CH)] = high
        work[1][pl.ds(base + r0, CH)] = low


def propagate(work, tabs, index):
    x_high, x_low, y_high, y_low, acc = work
    left_high, left_low, right_high, right_low = tabs
    acc[...] = dot3(left_high[index], left_low[index], x_high[...], x_low[...])
    for sl, s2, r0 in chunks():
        for ref, r, m in zip((y_high, y_low), split(acc[sl]), split(acc[s2])):
            ref[sl, 0:N] = r
            ref[s2, N : 2 * N] = r
            ref[s2, 0:N] = m
            ref[sl, N : 2 * N] = -m
    acc[...] = dot3(y_high[...], y_low[...], right_high[index], right_low[index])


def gather_patch(spot, p, own, near, far, out):
    mine_cols = own_cols(spot)
    for sl, _, r0 in chunks():
        mine_rows = own_rows(spot, r0)
        inner, outer = (mine_cols, mine_rows) if p % 2 == 0 else (mine_rows, mine_cols)
        for c in range(2):
            out[c, sl] = jnp.where(outer, jnp.where(inner, own[c, sl], near[c, sl]), far[c, sl])


def enter_slice(work, patch, wave):
    for sl, _, r0 in chunks():
        pr, pi, wr, wi = wave[0, sl], wave[1, sl], patch[0, sl], patch[1, sl]
        put_field(work, r0, pr * wr - pi * wi, pr * wi + pi * wr)


def leave(work, wave):
    acc = work[4]
    for sl, s2, _ in chunks():
        wave[0, sl] = acc[sl]
        wave[1, sl] = acc[s2]


def leave_slice(work, spot, p, patch, wave, grad, sent, onward):
    acc = work[4]
    mine_cols = own_cols(spot)
    for sl, s2, r0 in chunks():
        mr, mi, pr, pi = acc[sl], acc[s2], wave[0, sl], wave[1, sl]
        keep = own_rows(spot, r0) if p % 2 == 0 else mine_cols
        for c, g in enumerate((pr * mr + pi * mi, pr * mi - pi * mr)):
            grad[c, sl] = g
            sent[c, sl] = jnp.where(keep, 0.0, g)
        if onward:
            wr, wi = patch[0, sl], patch[1, sl]
            put_field(work, r0, wr * mr + wi * mi, wr * mi - wi * mr)


def first_kernel(spot, *refs):
    own, near, far = refs[0:2], refs[2:4], refs[4:6]
    probe, tabs = refs[6], refs[7:11]
    patches, waves = refs[11:13], refs[13:16]
    work = refs[16:]
    for c in range(2):
        waves[0][c] = pltpu.roll(pltpu.roll(probe[c], spot[0], 0), spot[1], 1)
    for p in range(2):
        gather_patch(spot, p, own[p], near[p], far[p], patches[p])
        enter_slice(work, patches[p], waves[p])
        propagate(work, tabs, 0)
        leave(work, waves[p + 1])


def second_kernel(spot, *refs):
    own, near, far = refs[0:2], refs[2:4], refs[4:6]
    measured, wave, tabs = refs[6], refs[7], refs[8:12]
    patch, middle, grad, sent, state = refs[12:17]
    last = refs[17:19]
    work = refs[19:]
    for p in range(2):
        gather_patch(spot, p, own[p], near[p], far[p], (patch, last[0])[p])
    enter_slice(work, patch, wave)
    propagate(work, tabs, 0)
    leave(work, middle)
    enter_slice(work, last[0], middle)
    propagate(work, tabs, 2)
    acc = work[4]
    scale = 2.0 * spot[3].astype(F32)
    for sl, s2, r0 in chunks():
        sr, si = acc[sl], acc[s2]
        misfit = (sr * sr + si * si - measured[sl]) * scale
        put_field(work, r0, misfit * sr, misfit * si)
    propagate(work, tabs, 3)
    leave_slice(work, spot, 3, last[0], middle, grad, sent, True)
    state[0] = work[0][...]
    state[1] = work[1][...]


def back_kernel(p, onward, spot, *refs):
    state, wave = refs[0], refs[1]
    n = 2
    patch = None
    if onward:
        patch = refs[2]
        n = 3
    tabs = refs[n : n + 4]
    outs = refs[n + 4 :]
    grad, sent = outs[0], outs[1]
    work = outs[3:] if onward else outs[2:]
    work[0][...] = state[0]
    work[1][...] = state[1]
    propagate(work, tabs, 1)
    leave_slice(work, spot, p, patch, wave, grad, sent, onward)
    if onward:
        outs[2][0] = work[0][...]
        outs[2][1] = work[1][...]


STATE = jax.ShapeDtypeStruct((2, 2 * N, N), BF)


def call(kernel, outs, spot, args, scratch=()):
    room = (20 if scratch else 8) << 20
    return pl.pallas_call(
        kernel,
        out_shape=outs,
        in_specs=[SS] + [VS] * len(args),
        out_specs=[VS] * len(outs),
        scratch_shapes=list(scratch),
        compiler_params=pltpu.CompilerParams(vmem_limit_bytes=room),
    )(spot, *args)


def blend_kernel(by_rows, spot, own, near, out):
    mine_cols = own_cols(spot)
    for sl, _, r0 in chunks():
        mask = own_rows(spot, r0) if by_rows else mine_cols
        for c in range(2):
            out[c, sl] = jnp.where(mask, own[c, sl], near[c, sl])


def turn_kernel(p, spots, grad, came, sent, kept):
    here = [spots[i] for i in range(3)]
    there = [spots[4 + i] for i in range(3)]
    cols, there_cols = own_cols(here), own_cols(there)
    for sl, _, r0 in chunks():
        rows = own_rows(here, r0)
        if p % 2 == 0:
            first, second, mask = rows, cols, there_cols
        else:
            first, second, mask = cols, rows, own_rows(there, r0)
        for c in range(2):
            g = jnp.where(first, grad[c, sl], 0.0)
            v = came[c, sl]
            sent[c, sl] = jnp.where(second, 0.0, g) + jnp.where(mask, 0.0, v)
            kept[c, sl] = jnp.where(second, g, 0.0) + jnp.where(mask, v, 0.0)


def merge_kernel(spot, *refs):
    kept, went = refs[0:4], refs[4:8]
    stay, leave_ = refs[8], refs[9]
    upper = spot[2] == 1
    for q in range(2):
        for c in range(2):
            for sl, _, _ in chunks():
                low = kept[q][c, sl] + went[q][c, sl]
                high = kept[q + 2][c, sl] + went[q + 2][c, sl]
                stay[q, c, sl] = jnp.where(upper, high, low)
                leave_[q, c, sl] = jnp.where(upper, low, high)


def order_kernel(spot, mine, other, *outs):
    upper = spot[2] == 1
    for k in range(4):
        for c in range(2):
            for sl, _, _ in chunks():
                a, b = mine[k % 2, c, sl], other[k % 2, c, sl]
                outs[k][c, sl] = jnp.where(upper, b, a) if k < 2 else jnp.where(upper, a, b)


def moved(t, dx, dy):
    return ((t // GX + dy) % ROWS) * GX + (t % GX + dx) % GX


def pairs_of(*per_core):
    out = []
    for d, step in enumerate(per_core):
        if step is not None:
            out += [(d * TILES + t, d * TILES + moved(t, *step)) for t in range(TILES)]
    return out


GATHER = (pairs_of((-1, 0), (1, 0)), pairs_of((0, -1), (0, 1)))
SCATTER = (pairs_of((1, 0), (-1, 0)), pairs_of((0, 1), (0, -1)))
INFO = (pairs_of((1, 0), (1, 0)), pairs_of((0, 1), (0, 1)))
DIAGONAL = pairs_of(None, (1, 1))
SWAP = [(d * TILES + t, (1 - d) * TILES + t) for d in range(2) for t in range(TILES)]


def permute(block, pairs):
    return lax.ppermute(block, ("depth", "tiles"), pairs)


def fourier():
    row = lax.broadcasted_iota(jnp.int32, (N, N), 0)
    col = lax.broadcasted_iota(jnp.int32, (N, N), 1)
    phase = (row * col % N).astype(F32) * (2.0 * math.pi / N)
    scale = 1.0 / math.sqrt(N)
    return jnp.stack([jnp.cos(phase) * scale, -jnp.sin(phase) * scale])


def step(transmission, illumination, fresnel_taps, intensity, offsets, counts):
    core = lax.axis_index("depth").astype(jnp.int32)
    mine = transmission[:, :, 0]
    other = permute(mine, SWAP)
    alive = (core < counts[0]).astype(jnp.int32)
    info = jnp.concatenate([jnp.where(core == 0, offsets[0, 0], offsets[0, 1]), core[None], alive[None]])
    left = permute(info, INFO[0])
    up = permute(info, INFO[1])
    upleft = permute(info, DIAGONAL)
    here = jnp.where(core == 0, info, upleft)
    at_y = jnp.where(core == 0, up, left)
    at_x = jnp.where(core == 0, left, up)
    own = call(order_kernel, [FIELD] * 4, info, [mine, other])

    near = [permute(own[p], GATHER[p % 2]) for p in range(4)]
    shared = permute(intensity[0, 1], DIAGONAL)
    measured = jnp.where(core == 0, intensity[0, 0], shared)
    far = []
    for p in range(4):
        mixed, = call(functools.partial(blend_kernel, p % 2 == 1), [FIELD], (at_y, at_x)[p % 2], [own[p], near[p]])
        far.append(permute(mixed, GATHER[1 - p % 2]))

    tabs = tables(here, tap_rows(fresnel_taps), fourier())
    _, patch1, wave0, wave1, wave2 = call(
        first_kernel, [FIELD] * 5, here, [*own[:2], *near[:2], *far[:2], illumination, *tabs], WORK
    )
    patch2, _, grad3, sent3, state = call(
        second_kernel, [FIELD] * 4 + [STATE], here, [*own[2:], *near[2:], *far[2:], measured, wave2, *tabs],
        [pltpu.VMEM((2, N, N), F32)] * 2 + WORK
    )
    grads = [None, None, None, grad3]
    came = [None, None, None, permute(sent3, SCATTER[0])]
    for p, wave, patch in ((2, wave2, patch2), (1, wave1, patch1), (0, wave0, None)):
        onward = p > 0
        outs = call(
            functools.partial(back_kernel, p, onward), [FIELD] * 2 + [STATE] * onward, here,
            [state, wave] + [patch] * onward + list(tabs), WORK
        )
        grads[p] = outs[0]
        came[p] = permute(outs[1], SCATTER[1 - p % 2])
        state = outs[2] if onward else None
    kept, went = [None] * 4, [None] * 4
    for p in (3, 2, 1, 0):
        spots = jnp.concatenate([here, (at_y, at_x)[p % 2]])
        sent, kept[p] = call(functools.partial(turn_kernel, p), [FIELD] * 2, spots, [grads[p], came[p]])
        went[p] = permute(sent, SCATTER[p % 2])
    pair = jax.ShapeDtypeStruct((2, 2, N, N), F32)
    stay, leaving = call(merge_kernel, [pair] * 2, here, [*kept, *went])
    back = permute(leaving, SWAP)
    return (stay + back)[:, :, None]


def solution(mesh):
    placed = (
        P("depth", None, "tiles", None, None),
        P(),
        P(),
        P("tiles", None, None, None),
        P("tiles", None, None),
        P("tiles"),
    )
    return jax.shard_map(
        step,
        mesh=mesh,
        in_specs=placed,
        out_specs=P("depth", None, "tiles", None, None),
        check_vma=False,
    )
```

```python
import functools
import math

import jax
import jax.numpy as jnp
from jax import lax
from jax.experimental import pallas as pl
from jax.experimental.pallas import tpu as pltpu
from jax.sharding import PartitionSpec as P

GX = 4
ROWS = 16
TILES = 64
N = 256
CH = 32
BF = jnp.bfloat16
F32 = jnp.float32
FIELD = jax.ShapeDtypeStruct((2, N, N), F32)
VS = pl.BlockSpec(memory_space=pltpu.VMEM)
SS = pl.BlockSpec(memory_space=pltpu.SMEM)


def split(x):
    high = x.astype(BF)
    return high, (x - high.astype(F32)).astype(BF)


def dot3(left_high, left_low, right_high, right_low):
    dot = functools.partial(jnp.dot, preferred_element_type=F32)
    return dot(left_high, right_high) + dot(left_high, right_low) + dot(left_low, right_high)


def put_left(refs, index, re, im):
    for ref, r, m in zip(refs, split(re), split(im)):
        ref[index, 0:N, 0:N] = r
        ref[index, N : 2 * N, N : 2 * N] = r
        ref[index, N : 2 * N, 0:N] = m
        ref[index, 0:N, N : 2 * N] = -m


def put_right(refs, index, re, im):
    for ref, r, m in zip(refs, split(re), split(im)):
        ref[index, 0:N] = r
        ref[index, N : 2 * N] = m


def tables_kernel(spot, taps, dft, left_high, left_low, right_high, right_low, a_high, a_low, b_high, b_low):
    left = (left_high, left_low)
    right = (right_high, right_low)
    a = (a_high, a_low)
    b = (b_high, b_low)
    row = lax.broadcasted_iota(jnp.int32, (N, N), 0)
    col = lax.broadcasted_iota(jnp.int32, (N, N), 1)

    def circulant(k):
        base = jnp.broadcast_to(taps[k : k + 1, :], (N, N))
        return pltpu.roll(base, 0, 1, stride=1, stride_axis=0)

    rings = [circulant(k) for k in range(4)]
    fr, fi = dft[0], dft[1]

    def bands(shift):
        inside = jnp.abs(((row - shift) & (N - 1)) - ((col - shift) & (N - 1))) <= 15
        return [jnp.where(inside, ring, 0.0) for ring in rings]

    def multiply():
        m = dot3(a_high[0], a_low[0], b_high[0], b_low[0])
        return m[:N], m[N:]

    tr, ti, ttr, tti = bands(spot[0])
    put_left(left, 0, tr, ti)
    put_left(left, 1, ttr, -tti)
    put_left(a, 0, fr, fi)
    put_right(b, 0, tr, ti)
    mr, mi = multiply()
    put_left(left, 2, mr, mi)
    put_left(a, 0, ttr, tti)
    put_right(b, 0, fr, fi)
    mr, mi = multiply()
    put_left(left, 3, mr, -mi)
    tr, ti, ttr, tti = bands(spot[1])
    put_right(right, 0, ttr, tti)
    put_right(right, 1, tr, -ti)
    put_left(a, 0, ttr, tti)
    mr, mi = multiply()
    put_right(right, 2, mr, mi)
    put_left(a, 0, fr, fi)
    put_right(b, 0, tr, ti)
    mr, mi = multiply()
    put_right(right, 3, mr, -mi)


def tables(spot, taps, dft):
    return pl.pallas_call(
        tables_kernel,
        out_shape=[jax.ShapeDtypeStruct((4, 2 * N, 2 * N), BF)] * 2
        + [jax.ShapeDtypeStruct((4, 2 * N, N), BF)] * 2,
        in_specs=[SS, VS, VS],
        out_specs=[VS] * 4,
        scratch_shapes=[pltpu.VMEM((1, 2 * N, 2 * N), BF)] * 2 + [pltpu.VMEM((1, 2 * N, N), BF)] * 2,
        compiler_params=pltpu.CompilerParams(vmem_limit_bytes=12 << 20),
        name="tables",
    )(spot, taps, dft)


def tap_rows(taps):
    rows = jnp.concatenate([taps, taps[:, ::-1]], 0)
    rows = jnp.pad(rows, ((0, 4), (0, N - rows.shape[1])))
    return jnp.roll(rows, -15, 1)


def chunks():
    return [(pl.ds(r0, CH), pl.ds(N + r0, CH), r0) for r0 in range(0, N, CH)]


def own_rows(spot, r0):
    row = lax.broadcasted_iota(jnp.int32, (CH, N), 0) + r0
    return ((row >= spot[0]).astype(jnp.int32) ^ spot[2]) == 1


def own_cols(spot):
    col = lax.broadcasted_iota(jnp.int32, (CH, N), 1)
    return ((col >= spot[1]).astype(jnp.int32) ^ spot[2]) == 1


WORK = (
    [pltpu.VMEM((2 * N, N), BF)] * 2
    + [pltpu.VMEM((2 * N, 2 * N), BF)] * 2
    + [pltpu.VMEM((2 * N, N), F32)]
)


def put_field(work, r0, re, im):
    for base, part in ((0, re), (N, im)):
        high, low = split(part)
        work[0][pl.ds(base + r0, CH)] = high
        work[1][pl.ds(base + r0, CH)] = low


def propagate(work, tabs, index):
    x_high, x_low, y_high, y_low, acc = work
    left_high, left_low, right_high, right_low = tabs
    half = N // 2
    spans = [(pl.ds(h * half, half), pl.ds(N + h * half, half)) for h in range(2)]
    for sl, s2 in spans:
        re = dot3(left_high[index, sl], left_low[index, sl], x_high[...], x_low[...])
        im = dot3(left_high[index, s2], left_low[index, s2], x_high[...], x_low[...])
        for ref, r, m in zip((y_high, y_low), split(re), split(im)):
            ref[sl, 0:N] = r
            ref[s2, N : 2 * N] = r
            ref[s2, 0:N] = m
            ref[sl, N : 2 * N] = -m
    for span in spans:
        for part in span:
            acc[part] = dot3(y_high[part], y_low[part], right_high[index], right_low[index])


def gather_patch(spot, p, inner, far, out):
    mine_cols = own_cols(spot)
    for sl, _, r0 in chunks():
        mask = own_rows(spot, r0) if p % 2 == 0 else mine_cols
        for c in range(2):
            out[c, sl] = jnp.where(mask, inner[c, sl], far[c, sl])


def enter_slice(work, patch, wave):
    for sl, _, r0 in chunks():
        pr, pi, wr, wi = wave[0, sl], wave[1, sl], patch[0, sl], patch[1, sl]
        put_field(work, r0, pr * wr - pi * wi, pr * wi + pi * wr)


def leave(work, wave):
    acc = work[4]
    for sl, s2, _ in chunks():
        wave[0, sl] = acc[sl]
        wave[1, sl] = acc[s2]


def leave_slice(work, spot, p, patch, wave, grad, sent, onward):
    acc = work[4]
    mine_cols = own_cols(spot)
    for sl, s2, r0 in chunks():
        mr, mi, pr, pi = acc[sl], acc[s2], wave[0, sl], wave[1, sl]
        keep = own_rows(spot, r0) if p % 2 == 0 else mine_cols
        for c, g in enumerate((pr * mr + pi * mi, pr * mi - pi * mr)):
            grad[c, sl] = g
            sent[c, sl] = jnp.where(keep, 0.0, g)
        if onward:
            wr, wi = patch[0, sl], patch[1, sl]
            put_field(work, r0, wr * mr + wi * mi, wr * mi - wi * mr)


def first_kernel(spot, *refs):
    inner, far = refs[0:2], refs[2:4]
    probe, tabs = refs[4], refs[5:9]
    patches, waves = refs[9:11], refs[11:14]
    work = refs[14:]
    for c in range(2):
        waves[0][c] = pltpu.roll(pltpu.roll(probe[c], spot[0], 0), spot[1], 1)
    for p in range(2):
        gather_patch(spot, p, inner[p], far[p], patches[p])
        enter_slice(work, patches[p], waves[p])
        propagate(work, tabs, 0)
        leave(work, waves[p + 1])


def second_kernel(spot, *refs):
    inner, far = refs[0:2], refs[2:4]
    wave, tabs = refs[4], refs[5:9]
    patches, middle, spectrum = refs[9:11], refs[11], refs[12]
    work = refs[13:]
    for p in range(2):
        gather_patch(spot, p, inner[p], far[p], patches[p])
    enter_slice(work, patches[0], wave)
    propagate(work, tabs, 0)
    leave(work, middle)
    enter_slice(work, patches[1], middle)
    propagate(work, tabs, 2)
    leave(work, spectrum)


def third_kernel(spot, *refs):
    spectrum, measured, shared, wave, patch, tabs = refs[0], refs[1], refs[2], refs[3], refs[4], refs[5:9]
    grad, sent, state = refs[9:12]
    work = refs[12:]
    upper = spot[2] == 1
    scale = 2.0 * spot[3].astype(F32)
    for sl, _, r0 in chunks():
        sr, si = spectrum[0, sl], spectrum[1, sl]
        target = jnp.where(upper, shared[sl], measured[sl])
        misfit = (sr * sr + si * si - target) * scale
        put_field(work, r0, misfit * sr, misfit * si)
    propagate(work, tabs, 3)
    leave_slice(work, spot, 3, patch, wave, grad, sent, True)
    state[0] = work[0][...]
    state[1] = work[1][...]


def back_kernel(p, onward, spot, *refs):
    state, wave = refs[0], refs[1]
    n = 2
    patch = None
    if onward:
        patch = refs[2]
        n = 3
    tabs = refs[n : n + 4]
    outs = refs[n + 4 :]
    grad, sent = outs[0], outs[1]
    work = outs[3:] if onward else outs[2:]
    work[0][...] = state[0]
    work[1][...] = state[1]
    propagate(work, tabs, 1)
    leave_slice(work, spot, p, patch, wave, grad, sent, onward)
    if onward:
        outs[2][0] = work[0][...]
        outs[2][1] = work[1][...]


STATE = jax.ShapeDtypeStruct((2, 2 * N, N), BF)


def call(kernel, outs, spot, args, scratch=()):
    room = (12 if scratch else 6) << 20
    return pl.pallas_call(
        kernel,
        out_shape=outs,
        in_specs=[SS] + [VS] * len(args),
        out_specs=[VS] * len(outs),
        scratch_shapes=list(scratch),
        compiler_params=pltpu.CompilerParams(vmem_limit_bytes=room),
    )(spot, *args)


def blend_kernel(by_rows, spots, own, near, mixed, inner):
    here = [spots[i] for i in range(3)]
    there = [spots[4 + i] for i in range(3)]
    for sl, _, r0 in chunks():
        for spot, out in ((there, mixed), (here, inner)):
            mask = own_rows(spot, r0) if by_rows else own_cols(spot)
            for c in range(2):
                out[c, sl] = jnp.where(mask, own[c, sl], near[c, sl])


def turn_kernel(p, spots, grad, came, sent, kept):
    here = [spots[i] for i in range(3)]
    there = [spots[4 + i] for i in range(3)]
    cols, there_cols = own_cols(here), own_cols(there)
    for sl, _, r0 in chunks():
        rows = own_rows(here, r0)
        if p % 2 == 0:
            first, second, mask = rows, cols, there_cols
        else:
            first, second, mask = cols, rows, own_rows(there, r0)
        for c in range(2):
            g = jnp.where(first, grad[c, sl], 0.0)
            v = came[c, sl]
            sent[c, sl] = jnp.where(second, 0.0, g) + jnp.where(mask, 0.0, v)
            kept[c, sl] = jnp.where(second, g, 0.0) + jnp.where(mask, v, 0.0)


def merge_kernel(spot, *refs):
    kept, went, stay, leaving = refs[0:4], refs[4:6], refs[6], refs[7]
    upper = spot[2] == 1
    for q in range(2):
        for c in range(2):
            for sl, _, _ in chunks():
                low = kept[q][c, sl]
                high = kept[q + 2][c, sl] + went[q][c, sl]
                stay[q, c, sl] = jnp.where(upper, high, low)
                leaving[q, c, sl] = jnp.where(upper, low, high)


def final_kernel(spot, stay, back, *refs):
    out = refs[4]
    for q in range(2):
        for c in range(2):
            for sl, _, _ in chunks():
                out[q, c, sl] = (stay[q, c, sl] + back[q, c, sl]) + (refs[q][c, sl] + refs[q + 2][c, sl])


def order_kernel(spot, mine, other, *outs):
    upper = spot[2] == 1
    for k in range(4):
        for c in range(2):
            for sl, _, _ in chunks():
                a, b = mine[k % 2, c, sl], other[k % 2, c, sl]
                outs[k][c, sl] = jnp.where(upper, b, a) if k < 2 else jnp.where(upper, a, b)


def moved(t, dx, dy):
    return ((t // GX + dy) % ROWS) * GX + (t % GX + dx) % GX


def pairs_of(*per_core):
    out = []
    for d, step in enumerate(per_core):
        if step is not None:
            out += [(d * TILES + t, d * TILES + moved(t, *step)) for t in range(TILES)]
    return out


GATHER = (pairs_of((-1, 0), (1, 0)), pairs_of((0, -1), (0, 1)))
SCATTER = (pairs_of((1, 0), (-1, 0)), pairs_of((0, 1), (0, -1)))
INFO = (pairs_of((1, 0), (1, 0)), pairs_of((0, 1), (0, 1)))
STRAIGHT = [[(a, b) for a, b in way if a < TILES] for way in SCATTER]
CROSSED = [[(a, b - TILES) for a, b in way if a >= TILES] for way in SCATTER]
DIAGONAL = pairs_of(None, (1, 1))
SWAP = [(d * TILES + t, (1 - d) * TILES + t) for d in range(2) for t in range(TILES)]


def permute(block, pairs):
    return lax.ppermute(block, ("depth", "tiles"), pairs)


def fourier():
    row = lax.broadcasted_iota(jnp.int32, (N, N), 0)
    col = lax.broadcasted_iota(jnp.int32, (N, N), 1)
    phase = (row * col % N).astype(F32) * (2.0 * math.pi / N)
    scale = 1.0 / math.sqrt(N)
    return jnp.stack([jnp.cos(phase) * scale, -jnp.sin(phase) * scale])


def step(transmission, illumination, fresnel_taps, intensity, offsets, counts):
    core = lax.axis_index("depth").astype(jnp.int32)
    mine = transmission[:, :, 0]
    other = permute(mine, SWAP)
    alive = (core < counts[0]).astype(jnp.int32)
    info = jnp.concatenate([jnp.where(core == 0, offsets[0, 0], offsets[0, 1]), core[None], alive[None]])
    left = permute(info, INFO[0])
    above = permute(jnp.concatenate([info, left]), INFO[1])
    up, upleft = above[:4], above[4:]
    here = jnp.where(core == 0, info, upleft)
    at_y = jnp.where(core == 0, up, left)
    at_x = jnp.where(core == 0, left, up)
    own = call(order_kernel, [FIELD] * 4, info, [mine, other])

    near = [permute(own[p], GATHER[p % 2]) for p in range(4)]
    shared = permute(intensity[0, 1], DIAGONAL)
    far, inner = [], []
    both = [jnp.concatenate([here, spot]) for spot in (at_y, at_x)]
    for p in range(4):
        mixed, kept = call(functools.partial(blend_kernel, p % 2 == 1), [FIELD] * 2, both[p % 2], [own[p], near[p]])
        inner.append(kept)
        far.append(permute(mixed, GATHER[1 - p % 2]))

    tabs = tables(here, tap_rows(fresnel_taps), fourier())
    _, patch1, wave0, wave1, wave2 = call(
        first_kernel, [FIELD] * 5, here, [*inner[:2], *far[:2], illumination, *tabs], WORK
    )
    patch2, patch3, wave3, spectrum = call(second_kernel, [FIELD] * 4, here, [*inner[2:], *far[2:], wave2, *tabs], WORK)
    grad3, sent3, state = call(
        third_kernel, [FIELD] * 2 + [STATE], here, [spectrum, intensity[0, 0], shared, wave3, patch3, *tabs], WORK
    )
    grads = [None, None, None, grad3]
    came = [None, None, None, permute(sent3, SCATTER[0])]
    for p, wave, patch in ((2, wave2, patch2), (1, wave1, patch1), (0, wave0, None)):
        onward = p > 0
        outs = call(
            functools.partial(back_kernel, p, onward), [FIELD] * 2 + [STATE] * onward, here,
            [state, wave] + [patch] * onward + list(tabs), WORK
        )
        grads[p] = outs[0]
        came[p] = permute(outs[1], SCATTER[1 - p % 2])
        state = outs[2] if onward else None
    kept, went = [None] * 4, [None] * 4
    for p in (3, 2, 1, 0):
        sent, kept[p] = call(functools.partial(turn_kernel, p), [FIELD] * 2, both[p % 2], [grads[p], came[p]])
        if p > 1:
            went[p] = permute(sent, SCATTER[p % 2])
        else:
            went[p] = [permute(sent, way[p % 2]) for way in (STRAIGHT, CROSSED)]
    pair = jax.ShapeDtypeStruct((2, 2, N, N), F32)
    stay, leaving = call(merge_kernel, [pair] * 2, here, [*kept, went[2], went[3]])
    back = permute(leaving, SWAP)
    last = [went[0][0], went[1][0], went[0][1], went[1][1]]
    out, = call(final_kernel, [pair], here, [stay, back, *last])
    return out[:, :, None]


def solution(mesh):
    placed = (
        P("depth", None, "tiles", None, None),
        P(),
        P(),
        P("tiles", None, None, None),
        P("tiles", None, None),
        P("tiles"),
    )
    return jax.shard_map(
        step,
        mesh=mesh,
        in_specs=placed,
        out_specs=P("depth", None, "tiles", None, None),
        check_vma=False,
    )
```

```python
import functools
import math

import jax
import jax.numpy as jnp
from jax import lax
from jax.experimental import pallas as pl
from jax.experimental.pallas import tpu as pltpu
from jax.sharding import PartitionSpec as P

GX = 4
ROWS = 16
TILES = 64
N = 256
CH = 32
BF = jnp.bfloat16
F32 = jnp.float32
FIELD = jax.ShapeDtypeStruct((2, N, N), F32)
VS = pl.BlockSpec(memory_space=pltpu.VMEM)
SS = pl.BlockSpec(memory_space=pltpu.SMEM)


def split(x):
    high = x.astype(BF)
    return high, (x - high.astype(F32)).astype(BF)


def dot3(left_high, left_low, right_high, right_low):
    dot = functools.partial(jnp.dot, preferred_element_type=F32)
    return dot(left_high, right_high) + dot(left_high, right_low) + dot(left_low, right_high)


def put_left(refs, index, re, im):
    for ref, r, m in zip(refs, split(re), split(im)):
        ref[index, 0:N, 0:N] = r
        ref[index, N : 2 * N, N : 2 * N] = r
        ref[index, N : 2 * N, 0:N] = m
        ref[index, 0:N, N : 2 * N] = -m


def put_right(refs, index, re, im):
    for ref, r, m in zip(refs, split(re), split(im)):
        ref[index, 0:N] = r
        ref[index, N : 2 * N] = m


def tables_kernel(spot, taps, dft, left_high, left_low, right_high, right_low, a_high, a_low, b_high, b_low):
    left = (left_high, left_low)
    right = (right_high, right_low)
    a = (a_high, a_low)
    b = (b_high, b_low)
    row = lax.broadcasted_iota(jnp.int32, (N, N), 0)
    col = lax.broadcasted_iota(jnp.int32, (N, N), 1)

    def circulant(k):
        base = jnp.broadcast_to(taps[k : k + 1, :], (N, N))
        return pltpu.roll(base, 0, 1, stride=1, stride_axis=0)

    rings = [circulant(k) for k in range(4)]
    fr, fi = dft[0], dft[1]

    def bands(shift):
        inside = jnp.abs(((row - shift) & (N - 1)) - ((col - shift) & (N - 1))) <= 15
        return [jnp.where(inside, ring, 0.0) for ring in rings]

    def multiply():
        m = dot3(a_high[0], a_low[0], b_high[0], b_low[0])
        return m[:N], m[N:]

    tr, ti, ttr, tti = bands(spot[0])
    put_left(left, 0, tr, ti)
    put_left(left, 1, ttr, -tti)
    put_left(a, 0, fr, fi)
    put_right(b, 0, tr, ti)
    mr, mi = multiply()
    put_left(left, 2, mr, mi)
    put_left(a, 0, ttr, tti)
    put_right(b, 0, fr, fi)
    mr, mi = multiply()
    put_left(left, 3, mr, -mi)
    tr, ti, ttr, tti = bands(spot[1])
    put_right(right, 0, ttr, tti)
    put_right(right, 1, tr, -ti)
    put_left(a, 0, ttr, tti)
    mr, mi = multiply()
    put_right(right, 2, mr, mi)
    put_left(a, 0, fr, fi)
    put_right(b, 0, tr, ti)
    mr, mi = multiply()
    put_right(right, 3, mr, -mi)


def tables(spot, taps, dft):
    return pl.pallas_call(
        tables_kernel,
        out_shape=[jax.ShapeDtypeStruct((4, 2 * N, 2 * N), BF)] * 2
        + [jax.ShapeDtypeStruct((4, 2 * N, N), BF)] * 2,
        in_specs=[SS, VS, VS],
        out_specs=[VS] * 4,
        scratch_shapes=[pltpu.VMEM((1, 2 * N, 2 * N), BF)] * 2 + [pltpu.VMEM((1, 2 * N, N), BF)] * 2,
        compiler_params=pltpu.CompilerParams(vmem_limit_bytes=12 << 20),
        name="tables",
    )(spot, taps, dft)


def tap_rows(taps):
    rows = jnp.concatenate([taps, taps[:, ::-1]], 0)
    rows = jnp.pad(rows, ((0, 4), (0, N - rows.shape[1])))
    return jnp.roll(rows, -15, 1)


def chunks():
    return [(pl.ds(r0, CH), pl.ds(N + r0, CH), r0) for r0 in range(0, N, CH)]


def own_rows(spot, r0):
    row = lax.broadcasted_iota(jnp.int32, (CH, N), 0) + r0
    return ((row >= spot[0]).astype(jnp.int32) ^ spot[2]) == 1


def own_cols(spot):
    col = lax.broadcasted_iota(jnp.int32, (CH, N), 1)
    return ((col >= spot[1]).astype(jnp.int32) ^ spot[2]) == 1


WORK = (
    [pltpu.VMEM((2 * N, N), BF)] * 2
    + [pltpu.VMEM((2 * N, 2 * N), BF)] * 2
    + [pltpu.VMEM((2 * N, N), F32)]
)


def put_field(work, r0, re, im):
    for base, part in ((0, re), (N, im)):
        high, low = split(part)
        work[0][pl.ds(base + r0, CH)] = high
        work[1][pl.ds(base + r0, CH)] = low


def propagate(work, tabs, index):
    x_high, x_low, y_high, y_low, acc = work
    left_high, left_low, right_high, right_low = tabs
    half = N // 2
    spans = [(pl.ds(h * half, half), pl.ds(N + h * half, half)) for h in range(2)]
    for sl, s2 in spans:
        re = dot3(left_high[index, sl], left_low[index, sl], x_high[...], x_low[...])
        im = dot3(left_high[index, s2], left_low[index, s2], x_high[...], x_low[...])
        for ref, r, m in zip((y_high, y_low), split(re), split(im)):
            ref[sl, 0:N] = r
            ref[s2, N : 2 * N] = r
            ref[s2, 0:N] = m
            ref[sl, N : 2 * N] = -m
    for span in spans:
        for part in span:
            acc[part] = dot3(y_high[part], y_low[part], right_high[index], right_low[index])


def gather_patch(spot, p, inner, far, out):
    mine_cols = own_cols(spot)
    for sl, _, r0 in chunks():
        mask = own_rows(spot, r0) if p % 2 == 0 else mine_cols
        for c in range(2):
            out[c, sl] = jnp.where(mask, inner[c, sl], far[c, sl])


def enter_slice(work, patch, wave):
    for sl, _, r0 in chunks():
        pr, pi, wr, wi = wave[0, sl], wave[1, sl], patch[0, sl], patch[1, sl]
        put_field(work, r0, pr * wr - pi * wi, pr * wi + pi * wr)


def leave(work, wave):
    acc = work[4]
    for sl, s2, _ in chunks():
        wave[0, sl] = acc[sl]
        wave[1, sl] = acc[s2]


def leave_slice(work, spot, p, patch, wave, grad, sent, onward):
    acc = work[4]
    mine_cols = own_cols(spot)
    for sl, s2, r0 in chunks():
        mr, mi, pr, pi = acc[sl], acc[s2], wave[0, sl], wave[1, sl]
        keep = own_rows(spot, r0) if p % 2 == 0 else mine_cols
        for c, g in enumerate((pr * mr + pi * mi, pr * mi - pi * mr)):
            grad[c, sl] = g
            sent[c, sl] = jnp.where(keep, 0.0, g)
        if onward:
            wr, wi = patch[0, sl], patch[1, sl]
            put_field(work, r0, wr * mr + wi * mi, wr * mi - wi * mr)


def first_kernel(spot, *refs):
    inner, far = refs[0:2], refs[2:4]
    probe, tabs = refs[4], refs[5:9]
    patches, waves = refs[9:11], refs[11:14]
    work = refs[14:]
    for c in range(2):
        waves[0][c] = pltpu.roll(pltpu.roll(probe[c], spot[0], 0), spot[1], 1)
    for p in range(2):
        gather_patch(spot, p, inner[p], far[p], patches[p])
        enter_slice(work, patches[p], waves[p])
        propagate(work, tabs, 0)
        leave(work, waves[p + 1])


def second_kernel(spot, *refs):
    inner, far = refs[0:2], refs[2:4]
    wave, tabs = refs[4], refs[5:9]
    patches, middle, spectrum = refs[9:11], refs[11], refs[12]
    work = refs[13:]
    for p in range(2):
        gather_patch(spot, p, inner[p], far[p], patches[p])
    enter_slice(work, patches[0], wave)
    propagate(work, tabs, 0)
    leave(work, middle)
    enter_slice(work, patches[1], middle)
    propagate(work, tabs, 2)
    leave(work, spectrum)


def third_kernel(spot, *refs):
    spectrum, measured, shared, wave, patch, tabs = refs[0], refs[1], refs[2], refs[3], refs[4], refs[5:9]
    grad, sent, state = refs[9:12]
    work = refs[12:]
    upper = spot[2] == 1
    scale = 2.0 * spot[3].astype(F32)
    for sl, _, r0 in chunks():
        sr, si = spectrum[0, sl], spectrum[1, sl]
        target = jnp.where(upper, shared[sl], measured[sl])
        misfit = (sr * sr + si * si - target) * scale
        put_field(work, r0, misfit * sr, misfit * si)
    propagate(work, tabs, 3)
    leave_slice(work, spot, 3, patch, wave, grad, sent, True)
    state[0] = work[0][...]
    state[1] = work[1][...]


def back_kernel(p, onward, spot, *refs):
    state, wave = refs[0], refs[1]
    n = 2
    patch = None
    if onward:
        patch = refs[2]
        n = 3
    tabs = refs[n : n + 4]
    outs = refs[n + 4 :]
    grad, sent = outs[0], outs[1]
    work = outs[3:] if onward else outs[2:]
    work[0][...] = state[0]
    work[1][...] = state[1]
    propagate(work, tabs, 1)
    leave_slice(work, spot, p, patch, wave, grad, sent, onward)
    if onward:
        outs[2][0] = work[0][...]
        outs[2][1] = work[1][...]


STATE = jax.ShapeDtypeStruct((2, 2 * N, N), BF)


def call(kernel, outs, spot, args, scratch=()):
    room = (12 if scratch else 6) << 20
    return pl.pallas_call(
        kernel,
        out_shape=outs,
        in_specs=[SS] + [VS] * len(args),
        out_specs=[VS] * len(outs),
        scratch_shapes=list(scratch),
        compiler_params=pltpu.CompilerParams(vmem_limit_bytes=room),
    )(spot, *args)


def blend_kernel(by_rows, spots, own, near, mixed, inner):
    here = [spots[i] for i in range(3)]
    there = [spots[4 + i] for i in range(3)]
    here_cols, there_cols = own_cols(here), own_cols(there)
    for sl, _, r0 in chunks():
        here_mask = own_rows(here, r0) if by_rows else here_cols
        there_mask = own_rows(there, r0) if by_rows else there_cols
        for c in range(2):
            u, v = own[c, sl], near[c, sl]
            mixed[c, sl] = jnp.where(there_mask, u, v)
            inner[c, sl] = jnp.where(here_mask, u, v)


def turn_kernel(parity, spots, *refs):
    grads, came, outs = refs[0:2], refs[2:4], refs[4:8]
    here = [spots[i] for i in range(3)]
    there = [spots[4 + i] for i in range(3)]
    cols, there_cols = own_cols(here), own_cols(there)
    upper = spots[2] == 1
    for sl, _, r0 in chunks():
        rows = own_rows(here, r0)
        if parity == 0:
            first, second, mask = rows, cols, there_cols
        else:
            first, second, mask = cols, rows, own_rows(there, r0)
        for c in range(2):
            sent, kept = [], []
            for grad, block in zip(grads, came):
                g = jnp.where(first, grad[c, sl], 0.0)
                v = block[c, sl]
                sent.append(jnp.where(second, 0.0, g) + jnp.where(mask, 0.0, v))
                kept.append(jnp.where(second, g, 0.0) + jnp.where(mask, v, 0.0))
            outs[0][c, sl] = jnp.where(upper, sent[1], sent[0])
            outs[1][c, sl] = jnp.where(upper, sent[0], sent[1])
            outs[2][c, sl] = jnp.where(upper, kept[1], kept[0])
            outs[3][c, sl] = jnp.where(upper, kept[0], kept[1])


def final_kernel(spot, *refs):
    out = refs[8]
    for q in range(2):
        for c in range(2):
            for sl, _, _ in chunks():
                a, b, x, y = (refs[4 * q + i][c, sl] for i in range(4))
                out[q, c, sl] = (a + b) + (x + y)


def load_kernel(spot, mine, *outs):
    for k in range(2):
        for c in range(2):
            for sl, _, _ in chunks():
                outs[k][c, sl] = mine[k, c, sl]


def order_kernel(spot, *refs):
    mine, other, outs = refs[0:2], refs[2], refs[3:7]
    upper = spot[2] == 1
    for k in range(4):
        for c in range(2):
            for sl, _, _ in chunks():
                a, b = mine[k % 2][c, sl], other[k % 2, c, sl]
                outs[k][c, sl] = jnp.where(upper, b, a) if k < 2 else jnp.where(upper, a, b)


def moved(t, dx, dy):
    return ((t // GX + dy) % ROWS) * GX + (t % GX + dx) % GX


def pairs_of(*per_core):
    out = []
    for d, step in enumerate(per_core):
        if step is not None:
            out += [(d * TILES + t, d * TILES + moved(t, *step)) for t in range(TILES)]
    return out


GATHER = (pairs_of((-1, 0), (1, 0)), pairs_of((0, -1), (0, 1)))
SCATTER = (pairs_of((1, 0), (-1, 0)), pairs_of((0, 1), (0, -1)))
INFO = (pairs_of((1, 0), (1, 0)), pairs_of((0, 1), (0, 1)))
CROSSED = [[(a, (b + TILES) % (2 * TILES)) for a, b in way] for way in SCATTER]
DIAGONAL = pairs_of(None, (1, 1))
SWAP = [(d * TILES + t, (1 - d) * TILES + t) for d in range(2) for t in range(TILES)]


def permute(block, pairs):
    return lax.ppermute(block, ("depth", "tiles"), pairs)


def fourier():
    row = lax.broadcasted_iota(jnp.int32, (N, N), 0)
    col = lax.broadcasted_iota(jnp.int32, (N, N), 1)
    phase = (row * col % N).astype(F32) * (2.0 * math.pi / N)
    scale = 1.0 / math.sqrt(N)
    return jnp.stack([jnp.cos(phase) * scale, -jnp.sin(phase) * scale])


def step(transmission, illumination, fresnel_taps, intensity, offsets, counts):
    core = lax.axis_index("depth").astype(jnp.int32)
    mine = transmission[:, :, 0]
    other = permute(mine, SWAP)
    alive = (core < counts[0]).astype(jnp.int32)
    info = jnp.concatenate([jnp.where(core == 0, offsets[0, 0], offsets[0, 1]), core[None], alive[None]])
    loaded = call(load_kernel, [FIELD] * 2, info, [mine])
    left = permute(info, INFO[0])
    up = permute(info, INFO[1])
    upleft = permute(info, DIAGONAL)
    here = jnp.where(core == 0, info, upleft)
    at_y = jnp.where(core == 0, up, left)
    at_x = jnp.where(core == 0, left, up)
    own = call(order_kernel, [FIELD] * 4, info, [*loaded, other])

    near = [permute(own[p], GATHER[p % 2]) for p in range(4)]
    shared = permute(intensity[0, 1], DIAGONAL)
    far, inner = [], []
    both = [jnp.concatenate([here, spot]) for spot in (at_y, at_x)]
    for p in range(4):
        mixed, kept = call(functools.partial(blend_kernel, p % 2 == 1), [FIELD] * 2, both[p % 2], [own[p], near[p]])
        inner.append(kept)
        far.append(permute(mixed, GATHER[1 - p % 2]))

    tabs = tables(here, tap_rows(fresnel_taps), fourier())
    _, patch1, wave0, wave1, wave2 = call(
        first_kernel, [FIELD] * 5, here, [*inner[:2], *far[:2], illumination, *tabs], WORK
    )
    patch2, patch3, wave3, spectrum = call(second_kernel, [FIELD] * 4, here, [*inner[2:], *far[2:], wave2, *tabs], WORK)
    grad3, sent3, state = call(
        third_kernel, [FIELD] * 2 + [STATE], here, [spectrum, intensity[0, 0], shared, wave3, patch3, *tabs], WORK
    )
    grads = [None, None, None, grad3]
    came = [None, None, None, permute(sent3, SCATTER[0])]
    for p, wave, patch in ((2, wave2, patch2), (1, wave1, patch1), (0, wave0, None)):
        onward = p > 0
        outs = call(
            functools.partial(back_kernel, p, onward), [FIELD] * 2 + [STATE] * onward, here,
            [state, wave] + [patch] * onward + list(tabs), WORK
        )
        grads[p] = outs[0]
        came[p] = permute(outs[1], SCATTER[1 - p % 2])
        state = outs[2] if onward else None
    parts = [None, None]
    for q in (1, 0):
        straight, cross, stay, leaving = call(
            functools.partial(turn_kernel, q), [FIELD] * 4, both[q], [grads[q], grads[q + 2], came[q], came[q + 2]]
        )
        parts[q] = [stay, permute(leaving, SWAP), permute(straight, SCATTER[q]), permute(cross, CROSSED[q])]
    out, = call(final_kernel, [jax.ShapeDtypeStruct((2, 2, N, N), F32)], here, parts[0] + parts[1])
    return out[:, :, None]


def solution(mesh):
    placed = (
        P("depth", None, "tiles", None, None),
        P(),
        P(),
        P("tiles", None, None, None),
        P("tiles", None, None),
        P("tiles"),
    )
    return jax.shard_map(
        step,
        mesh=mesh,
        in_specs=placed,
        out_specs=P("depth", None, "tiles", None, None),
        check_vma=False,
    )
```

```python
import functools
import math

import jax
import jax.numpy as jnp
from jax import lax
from jax.experimental import pallas as pl
from jax.experimental.pallas import tpu as pltpu
from jax.sharding import PartitionSpec as P

GX = 4
ROWS = 16
TILES = 64
N = 256
CH = 32
BF = jnp.bfloat16
F32 = jnp.float32
FIELD = jax.ShapeDtypeStruct((2, N, N), F32)
PAIR = jax.ShapeDtypeStruct((2, 2, N, N), F32)
ALL = jax.ShapeDtypeStruct((4, 2, N, N), F32)
VS = pl.BlockSpec(memory_space=pltpu.VMEM)
SS = pl.BlockSpec(memory_space=pltpu.SMEM)


def split(x):
    high = x.astype(BF)
    return high, (x - high.astype(F32)).astype(BF)


def dot3(left_high, left_low, right_high, right_low):
    dot = functools.partial(jnp.dot, preferred_element_type=F32)
    return dot(left_high, right_high) + dot(left_high, right_low) + dot(left_low, right_high)


def put_left(refs, index, re, im):
    for ref, r, m in zip(refs, split(re), split(im)):
        ref[index, 0:N, 0:N] = r
        ref[index, N : 2 * N, N : 2 * N] = r
        ref[index, N : 2 * N, 0:N] = m
        ref[index, 0:N, N : 2 * N] = -m


def put_right(refs, index, re, im):
    for ref, r, m in zip(refs, split(re), split(im)):
        ref[index, 0:N] = r
        ref[index, N : 2 * N] = m


def tables_kernel(spot, taps, dft, left_high, left_low, right_high, right_low, a_high, a_low, b_high, b_low):
    left = (left_high, left_low)
    right = (right_high, right_low)
    a = (a_high, a_low)
    b = (b_high, b_low)
    row = lax.broadcasted_iota(jnp.int32, (N, N), 0)
    col = lax.broadcasted_iota(jnp.int32, (N, N), 1)

    def circulant(k):
        base = jnp.broadcast_to(taps[k : k + 1, :], (N, N))
        return pltpu.roll(base, 0, 1, stride=1, stride_axis=0)

    rings = [circulant(k) for k in range(4)]
    fr, fi = dft[0], dft[1]

    def bands(shift):
        inside = jnp.abs(((row - shift) & (N - 1)) - ((col - shift) & (N - 1))) <= 15
        return [jnp.where(inside, ring, 0.0) for ring in rings]

    def multiply():
        m = dot3(a_high[0], a_low[0], b_high[0], b_low[0])
        return m[:N], m[N:]

    tr, ti, ttr, tti = bands(spot[0])
    put_left(left, 0, tr, ti)
    put_left(left, 1, ttr, -tti)
    put_left(a, 0, fr, fi)
    put_right(b, 0, tr, ti)
    mr, mi = multiply()
    put_left(left, 2, mr, mi)
    put_left(a, 0, ttr, tti)
    put_right(b, 0, fr, fi)
    mr, mi = multiply()
    put_left(left, 3, mr, -mi)
    tr, ti, ttr, tti = bands(spot[1])
    put_right(right, 0, ttr, tti)
    put_right(right, 1, tr, -ti)
    put_left(a, 0, ttr, tti)
    mr, mi = multiply()
    put_right(right, 2, mr, mi)
    put_left(a, 0, fr, fi)
    put_right(b, 0, tr, ti)
    mr, mi = multiply()
    put_right(right, 3, mr, -mi)


def tables(spot, taps, dft):
    return pl.pallas_call(
        tables_kernel,
        out_shape=[jax.ShapeDtypeStruct((4, 2 * N, 2 * N), BF)] * 2
        + [jax.ShapeDtypeStruct((4, 2 * N, N), BF)] * 2,
        in_specs=[SS, VS, VS],
        out_specs=[VS] * 4,
        scratch_shapes=[pltpu.VMEM((1, 2 * N, 2 * N), BF)] * 2 + [pltpu.VMEM((1, 2 * N, N), BF)] * 2,
        compiler_params=pltpu.CompilerParams(vmem_limit_bytes=12 << 20),
        name="tables",
    )(spot, taps, dft)


def tap_rows(taps):
    rows = jnp.concatenate([taps, taps[:, ::-1]], 0)
    rows = jnp.pad(rows, ((0, 4), (0, N - rows.shape[1])))
    return jnp.roll(rows, -15, 1)


def chunks():
    return [(pl.ds(r0, CH), pl.ds(N + r0, CH), r0) for r0 in range(0, N, CH)]


def own_rows(spot, r0):
    row = lax.broadcasted_iota(jnp.int32, (CH, N), 0) + r0
    return ((row >= spot[0]).astype(jnp.int32) ^ spot[2]) == 1


def own_cols(spot):
    col = lax.broadcasted_iota(jnp.int32, (CH, N), 1)
    return ((col >= spot[1]).astype(jnp.int32) ^ spot[2]) == 1


WORK = (
    [pltpu.VMEM((2 * N, N), BF)] * 2
    + [pltpu.VMEM((2 * N, 2 * N), BF)] * 2
    + [pltpu.VMEM((2 * N, N), F32)]
)


def put_field(work, r0, re, im):
    for base, part in ((0, re), (N, im)):
        high, low = split(part)
        work[0][pl.ds(base + r0, CH)] = high
        work[1][pl.ds(base + r0, CH)] = low


def propagate(work, tabs, index):
    x_high, x_low, y_high, y_low, acc = work
    left_high, left_low, right_high, right_low = tabs
    half = N // 2
    spans = [(pl.ds(h * half, half), pl.ds(N + h * half, half)) for h in range(2)]
    for sl, s2 in spans:
        re = dot3(left_high[index, sl], left_low[index, sl], x_high[...], x_low[...])
        im = dot3(left_high[index, s2], left_low[index, s2], x_high[...], x_low[...])
        for ref, r, m in zip((y_high, y_low), split(re), split(im)):
            ref[sl, 0:N] = r
            ref[s2, N : 2 * N] = r
            ref[s2, 0:N] = m
            ref[sl, N : 2 * N] = -m
    for span in spans:
        for part in span:
            acc[part] = dot3(y_high[part], y_low[part], right_high[index], right_low[index])


def enter_slice(work, patch, wave):
    for sl, _, r0 in chunks():
        pr, pi, wr, wi = wave[0, sl], wave[1, sl], patch[0, sl], patch[1, sl]
        put_field(work, r0, pr * wr - pi * wi, pr * wi + pi * wr)


def leave(work, wave):
    acc = work[4]
    for sl, s2, _ in chunks():
        wave[0, sl] = acc[sl]
        wave[1, sl] = acc[s2]


def leave_slice(work, spot, patch, wave, grad, sent_x, sent_y, onward):
    acc = work[4]
    mine_cols = own_cols(spot)
    for sl, s2, r0 in chunks():
        mr, mi, pr, pi = acc[sl], acc[s2], wave[0, sl], wave[1, sl]
        re = pr * mr + pi * mi
        im = pr * mi - pi * mr
        grad[0, sl] = re
        grad[1, sl] = im
        sent_x[sl] = jnp.where(mine_cols, 0.0, re)
        sent_y[sl] = jnp.where(own_rows(spot, r0), 0.0, im)
        if onward:
            wr, wi = patch[0, sl], patch[1, sl]
            put_field(work, r0, wr * mr + wi * mi, wr * mi - wi * mr)


def down_kernel(spot, *refs):
    mine, near_x, far_y, other, near_y, far_x = refs[0], refs[1], refs[2], refs[3], refs[4:6], refs[6:8]
    probe, tabs = refs[8], refs[9:13]
    patches, waves, spectrum = refs[13:16]
    work = refs[16:]
    core = spot[2]
    cols = own_cols(spot)
    for q in range(2):
        for sl, _, r0 in chunks():
            rows = own_rows(spot, r0)
            for c in range(2):
                inner = jnp.where(cols, mine[q, c, sl], near_x[q, c, sl])
                patches[2 * core + q, c, sl] = jnp.where(rows, inner, far_y[q, c, sl])
                inner = jnp.where(rows, other[q, c, sl], near_y[q][c, sl])
                patches[2 - 2 * core + q, c, sl] = jnp.where(cols, inner, far_x[q][c, sl])
    for c in range(2):
        waves[0, c] = pltpu.roll(pltpu.roll(probe[c], spot[0], 0), spot[1], 1)
    for k in range(4):
        enter_slice(work, patches.at[k], waves.at[k])
        propagate(work, tabs, 0 if k < 3 else 2)
        leave(work, waves.at[k + 1] if k < 3 else spectrum)


def save(work, state):
    state[0] = work[0][...]
    state[1] = work[1][...]


def turn_up_kernel(spot, *refs):
    spectrum, measured, shared, waves, patches, tabs = refs[0], refs[1], refs[2], refs[3], refs[4], refs[5:9]
    grad, sent_x, sent_y, state = refs[9:13]
    work = refs[13:]
    upper = spot[2] == 1
    scale = 2.0 * spot[3].astype(F32)
    for sl, _, r0 in chunks():
        sr, si = spectrum[0, sl], spectrum[1, sl]
        target = jnp.where(upper, shared[sl], measured[sl])
        misfit = (sr * sr + si * si - target) * scale
        put_field(work, r0, misfit * sr, misfit * si)
    for k in (3, 2):
        propagate(work, tabs, 3 if k == 3 else 1)
        leave_slice(work, spot, patches.at[k], waves.at[k], grad.at[k - 2], sent_x.at[k - 2], sent_y.at[k - 2], True)
    save(work, state)


def up_kernel(spot, *refs):
    state, waves, patches, tabs = refs[0], refs[1], refs[2], refs[3:7]
    grad, sent_x, sent_y = refs[7:10]
    work = refs[10:]
    work[0][...] = state[0]
    work[1][...] = state[1]
    for k in (1, 0):
        propagate(work, tabs, 1)
        leave_slice(work, spot, patches.at[k], waves.at[k], grad.at[k], sent_x.at[k], sent_y.at[k], k > 0)


STATE = jax.ShapeDtypeStruct((2, 2 * N, N), BF)


def call(kernel, outs, spot, args, scratch=()):
    room = (12 if scratch else 6) << 20
    return pl.pallas_call(
        kernel,
        out_shape=outs,
        in_specs=[SS] + [VS] * len(args),
        out_specs=[VS] * len(outs),
        scratch_shapes=list(scratch),
        compiler_params=pltpu.CompilerParams(vmem_limit_bytes=room),
    )(spot, *args)


def blend_kernel(by_rows, leads, spot, own, near, mixed):
    cols = own_cols(spot)
    for sl, _, r0 in chunks():
        mask = own_rows(spot, r0) if by_rows else cols
        for lead in leads:
            at = (*lead, sl)
            mixed[at] = jnp.where(mask, own[at], near[at])


def turn_kernel(channel, spots, *refs):
    grads, came, outs = refs[0:2], refs[2:4], refs[4:8]
    here = [spots[i] for i in range(3)]
    there = [spots[4 + i] for i in range(3)]
    cols, there_cols = own_cols(here), own_cols(there)
    upper = spots[2] == 1
    for sl, _, r0 in chunks():
        rows = own_rows(here, r0)
        if channel == 1:
            first, second, mask = rows, cols, there_cols
        else:
            first, second, mask = cols, rows, own_rows(there, r0)
        for q in range(2):
            sent, kept = [], []
            for grad, block in zip(grads, came):
                g = jnp.where(first, grad[q, channel, sl], 0.0)
                v = block[q, sl]
                sent.append(jnp.where(second, 0.0, g) + jnp.where(mask, 0.0, v))
                kept.append(jnp.where(second, g, 0.0) + jnp.where(mask, v, 0.0))
            outs[0][q, sl] = jnp.where(upper, sent[1], sent[0])
            outs[1][q, sl] = jnp.where(upper, sent[0], sent[1])
            outs[2][q, sl] = jnp.where(upper, kept[1], kept[0])
            outs[3][q, sl] = jnp.where(upper, kept[0], kept[1])


def final_kernel(spot, *refs):
    out = refs[8]
    for q in range(2):
        for c in range(2):
            for sl, _, _ in chunks():
                a, b, x, y = (refs[4 * c + i][q, sl] for i in range(4))
                out[q, c, sl] = (a + b) + (x + y)


def moved(t, dx, dy):
    return ((t // GX + dy) % ROWS) * GX + (t % GX + dx) % GX


def pairs_of(*per_core):
    out = []
    for d, step in enumerate(per_core):
        if step is not None:
            out += [(d * TILES + t, d * TILES + moved(t, *step)) for t in range(TILES)]
    return out


GATHER = (pairs_of((-1, 0), (1, 0)), pairs_of((0, -1), (0, 1)))
SCATTER = (pairs_of((1, 0), (-1, 0)), pairs_of((0, 1), (0, -1)))
INFO = (pairs_of((1, 0), (1, 0)), pairs_of((0, 1), (0, 1)))
CROSSED = [[(a, (b + TILES) % (2 * TILES)) for a, b in way] for way in SCATTER]
DIAGONAL = pairs_of(None, (1, 1))
SWAP = [(d * TILES + t, (1 - d) * TILES + t) for d in range(2) for t in range(TILES)]


def permute(block, pairs):
    return lax.ppermute(block, ("depth", "tiles"), pairs)


def fourier():
    row = lax.broadcasted_iota(jnp.int32, (N, N), 0)
    col = lax.broadcasted_iota(jnp.int32, (N, N), 1)
    phase = (row * col % N).astype(F32) * (2.0 * math.pi / N)
    scale = 1.0 / math.sqrt(N)
    return jnp.stack([jnp.cos(phase) * scale, -jnp.sin(phase) * scale])


def step(transmission, illumination, fresnel_taps, intensity, offsets, counts):
    core = lax.axis_index("depth").astype(jnp.int32)
    mine = transmission[:, :, 0]
    other = permute(mine, SWAP)
    near_x = permute(mine, GATHER[0])
    alive = (core < counts[0]).astype(jnp.int32)
    info = jnp.concatenate([jnp.where(core == 0, offsets[0, 0], offsets[0, 1]), core[None], alive[None]])
    left = permute(info, INFO[0])
    up = permute(info, INFO[1])
    upleft = permute(info, DIAGONAL)
    here = jnp.where(core == 0, info, upleft)
    at_y = jnp.where(core == 0, up, left)
    at_x = jnp.where(core == 0, left, up)
    near_y = [permute(other[q], GATHER[1]) for q in range(2)]

    leads = tuple((q, c) for q in range(2) for c in range(2))
    mixed, = call(functools.partial(blend_kernel, False, leads), [PAIR], at_y, [mine, near_x])
    far_y = permute(mixed, GATHER[1])
    far_x = []
    for q in range(2):
        mixed, = call(functools.partial(blend_kernel, True, ((0,), (1,))), [FIELD], at_x, [other[q], near_y[q]])
        far_x.append(permute(mixed, GATHER[0]))
    shared = permute(intensity[0, 1], DIAGONAL)

    tabs = tables(here, tap_rows(fresnel_taps), fourier())
    patches, waves, spectrum = call(
        down_kernel, [ALL, ALL, FIELD], here,
        [mine, near_x, far_y, other, *near_y, *far_x, illumination, *tabs], WORK
    )
    grad_high, x_high, y_high, state = call(
        turn_up_kernel, [PAIR, FIELD, FIELD, STATE], here,
        [spectrum, intensity[0, 0], shared, waves, patches, *tabs], WORK
    )
    came_high = [permute(x_high, SCATTER[0]), permute(y_high, SCATTER[1])]
    grad_low, x_low, y_low = call(up_kernel, [PAIR, FIELD, FIELD], here, [state, waves, patches, *tabs], WORK)
    came_low = [permute(x_low, SCATTER[0]), permute(y_low, SCATTER[1])]
    parts = []
    for channel, there in ((0, at_x), (1, at_y)):
        straight, cross, stay, leaving = call(
            functools.partial(turn_kernel, channel), [FIELD] * 4, jnp.concatenate([here, there]),
            [grad_low, grad_high, came_low[channel], came_high[channel]]
        )
        way = 1 - channel
        parts += [stay, permute(leaving, SWAP), permute(straight, SCATTER[way]), permute(cross, CROSSED[way])]
    out, = call(final_kernel, [PAIR], here, parts)
    return out[:, :, None]


def solution(mesh):
    placed = (
        P("depth", None, "tiles", None, None),
        P(),
        P(),
        P("tiles", None, None, None),
        P("tiles", None, None),
        P("tiles"),
    )
    return jax.shard_map(
        step,
        mesh=mesh,
        in_specs=placed,
        out_specs=P("depth", None, "tiles", None, None),
        check_vma=False,
    )
```

```python
import functools
import math

import jax
import jax.numpy as jnp
from jax import lax
from jax.experimental import pallas as pl
from jax.experimental.pallas import tpu as pltpu
from jax.sharding import PartitionSpec as P

GX = 4
ROWS = 16
TILES = 64
N = 256
CH = 32
BF = jnp.bfloat16
F32 = jnp.float32
FIELD = jax.ShapeDtypeStruct((2, N, N), F32)
PAIR = jax.ShapeDtypeStruct((2, 2, N, N), F32)
ALL = jax.ShapeDtypeStruct((4, 2, N, N), F32)
VS = pl.BlockSpec(memory_space=pltpu.VMEM)
SS = pl.BlockSpec(memory_space=pltpu.SMEM)


def split(x):
    high = x.astype(BF)
    return high, (x - high.astype(F32)).astype(BF)


def dot3(left_high, left_low, right_high, right_low):
    dot = functools.partial(jnp.dot, preferred_element_type=F32)
    return dot(left_high, right_high) + dot(left_high, right_low) + dot(left_low, right_high)


def put_left(refs, index, re, im):
    for ref, r, m in zip(refs, split(re), split(im)):
        ref[index, 0:N, 0:N] = r
        ref[index, N : 2 * N, N : 2 * N] = r
        ref[index, N : 2 * N, 0:N] = m
        ref[index, 0:N, N : 2 * N] = -m


def put_right(refs, index, re, im):
    for ref, r, m in zip(refs, split(re), split(im)):
        ref[index, 0:N] = r
        ref[index, N : 2 * N] = m


def tables_kernel(spot, taps, dft, left_high, left_low, right_high, right_low, a_high, a_low, b_high, b_low):
    left = (left_high, left_low)
    right = (right_high, right_low)
    a = (a_high, a_low)
    b = (b_high, b_low)
    row = lax.broadcasted_iota(jnp.int32, (N, N), 0)
    col = lax.broadcasted_iota(jnp.int32, (N, N), 1)

    def circulant(k):
        base = jnp.broadcast_to(taps[k : k + 1, :], (N, N))
        return pltpu.roll(base, 0, 1, stride=1, stride_axis=0)

    rings = [circulant(0), circulant(1)]
    rings += [ring.T for ring in rings]
    fr, fi = dft[0], dft[1]

    def bands(shift):
        inside = jnp.abs(((row - shift) & (N - 1)) - ((col - shift) & (N - 1))) <= 15
        return [jnp.where(inside, ring, 0.0) for ring in rings]

    def multiply():
        m = dot3(a_high[0], a_low[0], b_high[0], b_low[0])
        return m[:N], m[N:]

    tr, ti, ttr, tti = bands(spot[0])
    put_left(left, 0, tr, ti)
    put_left(left, 1, ttr, -tti)
    put_left(a, 0, fr, fi)
    put_right(b, 0, tr, ti)
    mr, mi = multiply()
    put_left(left, 2, mr, mi)
    put_left(a, 0, ttr, tti)
    put_right(b, 0, fr, fi)
    mr, mi = multiply()
    put_left(left, 3, mr, -mi)
    tr, ti, ttr, tti = bands(spot[1])
    put_right(right, 0, ttr, tti)
    put_right(right, 1, tr, -ti)
    put_left(a, 0, ttr, tti)
    mr, mi = multiply()
    put_right(right, 2, mr, mi)
    put_left(a, 0, fr, fi)
    put_right(b, 0, tr, ti)
    mr, mi = multiply()
    put_right(right, 3, mr, -mi)


def tables(spot, taps, dft):
    return pl.pallas_call(
        tables_kernel,
        out_shape=[jax.ShapeDtypeStruct((4, 2 * N, 2 * N), BF)] * 2
        + [jax.ShapeDtypeStruct((4, 2 * N, N), BF)] * 2,
        in_specs=[SS, VS, VS],
        out_specs=[VS] * 4,
        scratch_shapes=[pltpu.VMEM((1, 2 * N, 2 * N), BF)] * 2 + [pltpu.VMEM((1, 2 * N, N), BF)] * 2,
        compiler_params=pltpu.CompilerParams(vmem_limit_bytes=12 << 20),
        name="tables",
    )(spot, taps, dft)


def tap_rows(taps):
    rows = jnp.pad(taps, ((0, 6), (0, N - taps.shape[1])))
    return jnp.roll(rows, -15, 1)


def chunks():
    return [(pl.ds(r0, CH), pl.ds(N + r0, CH), r0) for r0 in range(0, N, CH)]


def own_rows(spot, r0):
    row = lax.broadcasted_iota(jnp.int32, (CH, N), 0) + r0
    return ((row >= spot[0]).astype(jnp.int32) ^ spot[2]) == 1


def own_cols(spot):
    col = lax.broadcasted_iota(jnp.int32, (CH, N), 1)
    return ((col >= spot[1]).astype(jnp.int32) ^ spot[2]) == 1


WORK = (
    [pltpu.VMEM((2 * N, N), BF)] * 2
    + [pltpu.VMEM((2 * N, 2 * N), BF)] * 2
    + [pltpu.VMEM((2 * N, N), F32)]
)


def put_field(work, r0, re, im):
    for base, part in ((0, re), (N, im)):
        high, low = split(part)
        work[0][pl.ds(base + r0, CH)] = high
        work[1][pl.ds(base + r0, CH)] = low


def propagate(work, tabs, index):
    x_high, x_low, y_high, y_low, acc = work
    left_high, left_low, right_high, right_low = tabs
    half = N // 2
    spans = [(pl.ds(h * half, half), pl.ds(N + h * half, half)) for h in range(2)]
    for sl, s2 in spans:
        re = dot3(left_high[index, sl], left_low[index, sl], x_high[...], x_low[...])
        im = dot3(left_high[index, s2], left_low[index, s2], x_high[...], x_low[...])
        for ref, r, m in zip((y_high, y_low), split(re), split(im)):
            ref[sl, 0:N] = r
            ref[s2, N : 2 * N] = r
            ref[s2, 0:N] = m
            ref[sl, N : 2 * N] = -m
    for span in spans:
        for part in span:
            acc[part] = dot3(y_high[part], y_low[part], right_high[index], right_low[index])


def enter_slice(work, patch, wave):
    for sl, _, r0 in chunks():
        pr, pi, wr, wi = wave[0, sl], wave[1, sl], patch[0, sl], patch[1, sl]
        put_field(work, r0, pr * wr - pi * wi, pr * wi + pi * wr)


def leave(work, wave):
    acc = work[4]
    for sl, s2, _ in chunks():
        wave[0, sl] = acc[sl]
        wave[1, sl] = acc[s2]


def leave_slice(work, spot, patch, wave, grad, sent_x, sent_y, onward):
    acc = work[4]
    mine_cols = own_cols(spot)
    for sl, s2, r0 in chunks():
        mr, mi, pr, pi = acc[sl], acc[s2], wave[0, sl], wave[1, sl]
        re = pr * mr + pi * mi
        im = pr * mi - pi * mr
        grad[0, sl] = re
        grad[1, sl] = im
        sent_x[sl] = jnp.where(mine_cols, 0.0, re)
        sent_y[sl] = jnp.where(own_rows(spot, r0), 0.0, im)
        if onward:
            wr, wi = patch[0, sl], patch[1, sl]
            put_field(work, r0, wr * mr + wi * mi, wr * mi - wi * mr)


def down_kernel(spot, *refs):
    mine, near_x, far_y, other, near_y, far_x = refs[0:6]
    probe, tabs = refs[6], refs[7:11]
    patches, waves, spectrum = refs[11:14]
    work = refs[14:]
    core = spot[2]
    cols = own_cols(spot)
    for q in range(2):
        for sl, _, r0 in chunks():
            rows = own_rows(spot, r0)
            for c in range(2):
                inner = jnp.where(cols, mine[q, c, sl], near_x[q, c, sl])
                patches[2 * core + q, c, sl] = jnp.where(rows, inner, far_y[q, c, sl])
                inner = jnp.where(rows, other[q, c, sl], near_y[q, c, sl])
                patches[2 - 2 * core + q, c, sl] = jnp.where(cols, inner, far_x[q, c, sl])
    for c in range(2):
        waves[0, c] = pltpu.roll(pltpu.roll(probe[c], spot[0], 0), spot[1], 1)
    for k in range(4):
        enter_slice(work, patches.at[k], waves.at[k])
        propagate(work, tabs, 0 if k < 3 else 2)
        leave(work, waves.at[k + 1] if k < 3 else spectrum)


def save(work, state):
    state[0] = work[0][...]
    state[1] = work[1][...]


def turn_up_kernel(spot, *refs):
    spectrum, measured, shared, waves, patches, tabs = refs[0], refs[1], refs[2], refs[3], refs[4], refs[5:9]
    grad, sent_x, sent_y, state = refs[9:13]
    work = refs[13:]
    upper = spot[2] == 1
    scale = 2.0 * spot[3].astype(F32)
    for sl, _, r0 in chunks():
        sr, si = spectrum[0, sl], spectrum[1, sl]
        target = jnp.where(upper, shared[sl], measured[sl])
        misfit = (sr * sr + si * si - target) * scale
        put_field(work, r0, misfit * sr, misfit * si)
    for k in (3, 2):
        propagate(work, tabs, 3 if k == 3 else 1)
        leave_slice(work, spot, patches.at[k], waves.at[k], grad.at[k - 2], sent_x.at[k - 2], sent_y.at[k - 2], True)
    save(work, state)


def up_kernel(spot, *refs):
    state, waves, patches, tabs = refs[0], refs[1], refs[2], refs[3:7]
    grad, sent_x, sent_y = refs[7:10]
    work = refs[10:]
    work[0][...] = state[0]
    work[1][...] = state[1]
    for k in (1, 0):
        propagate(work, tabs, 1)
        leave_slice(work, spot, patches.at[k], waves.at[k], grad.at[k], sent_x.at[k], sent_y.at[k], k > 0)


STATE = jax.ShapeDtypeStruct((2, 2 * N, N), BF)


def call(kernel, outs, spot, args, scratch=()):
    room = (12 if scratch else 6) << 20
    return pl.pallas_call(
        kernel,
        out_shape=outs,
        in_specs=[SS] + [VS] * len(args),
        out_specs=[VS] * len(outs),
        scratch_shapes=list(scratch),
        compiler_params=pltpu.CompilerParams(vmem_limit_bytes=room),
    )(spot, *args)


def load_kernel(spot, block, out):
    for q in range(2):
        for c in range(2):
            for sl, _, _ in chunks():
                out[q, c, sl] = block[q, c, sl]


def blend_kernel(by_rows, spot, own, near, mixed):
    cols = own_cols(spot)
    for sl, _, r0 in chunks():
        mask = own_rows(spot, r0) if by_rows else cols
        for q in range(2):
            for c in range(2):
                mixed[q, c, sl] = jnp.where(mask, own[q, c, sl], near[q, c, sl])


def turn_kernel(channel, spots, *refs):
    grads, came, outs = refs[0:2], refs[2:4], refs[4:8]
    here = [spots[i] for i in range(3)]
    there = [spots[4 + i] for i in range(3)]
    cols, there_cols = own_cols(here), own_cols(there)
    upper = spots[2] == 1
    for sl, _, r0 in chunks():
        rows = own_rows(here, r0)
        if channel == 1:
            first, second, mask = rows, cols, there_cols
        else:
            first, second, mask = cols, rows, own_rows(there, r0)
        for q in range(2):
            sent, kept = [], []
            for grad, block in zip(grads, came):
                g = jnp.where(first, grad[q, channel, sl], 0.0)
                v = block[q, sl]
                sent.append(jnp.where(second, 0.0, g) + jnp.where(mask, 0.0, v))
                kept.append(jnp.where(second, g, 0.0) + jnp.where(mask, v, 0.0))
            outs[0][q, sl] = jnp.where(upper, sent[1], sent[0])
            outs[1][q, sl] = jnp.where(upper, sent[0], sent[1])
            outs[2][q, sl] = jnp.where(upper, kept[1], kept[0])
            outs[3][q, sl] = jnp.where(upper, kept[0], kept[1])


def final_kernel(spot, *refs):
    out = refs[8]
    for q in range(2):
        for c in range(2):
            for sl, _, _ in chunks():
                a, b, x, y = (refs[4 * c + i][q, sl] for i in range(4))
                out[q, c, sl] = (a + b) + (x + y)


def moved(t, dx, dy):
    return ((t // GX + dy) % ROWS) * GX + (t % GX + dx) % GX


def pairs_of(*per_core):
    out = []
    for d, step in enumerate(per_core):
        if step is not None:
            out += [(d * TILES + t, d * TILES + moved(t, *step)) for t in range(TILES)]
    return out


GATHER = (pairs_of((-1, 0), (1, 0)), pairs_of((0, -1), (0, 1)))
SCATTER = (pairs_of((1, 0), (-1, 0)), pairs_of((0, 1), (0, -1)))
INFO = (pairs_of((1, 0), (1, 0)), pairs_of((0, 1), (0, 1)))
CROSSED = [[(a, (b + TILES) % (2 * TILES)) for a, b in way] for way in SCATTER]
DIAGONAL = pairs_of(None, (1, 1))
SWAP = [(d * TILES + t, (1 - d) * TILES + t) for d in range(2) for t in range(TILES)]


def permute(block, pairs):
    return lax.ppermute(block, ("depth", "tiles"), pairs)


def fourier():
    row = lax.broadcasted_iota(jnp.int32, (N, N), 0)
    col = lax.broadcasted_iota(jnp.int32, (N, N), 1)
    phase = (row * col % N).astype(F32) * (2.0 * math.pi / N)
    scale = 1.0 / math.sqrt(N)
    return jnp.stack([jnp.cos(phase) * scale, -jnp.sin(phase) * scale])


def step(transmission, illumination, fresnel_taps, intensity, offsets, counts):
    core = lax.axis_index("depth").astype(jnp.int32)
    mine = transmission[:, :, 0]
    other = permute(mine, SWAP)
    near_x = permute(mine, GATHER[0])
    alive = (core < counts[0]).astype(jnp.int32)
    info = jnp.concatenate([jnp.where(core == 0, offsets[0, 0], offsets[0, 1]), core[None], alive[None]])
    left = permute(info, INFO[0])
    up = permute(info, INFO[1])
    upleft = permute(info, DIAGONAL)
    here = jnp.where(core == 0, info, upleft)
    at_y = jnp.where(core == 0, up, left)
    at_x = jnp.where(core == 0, left, up)
    near_y = permute(other, GATHER[1])

    mine, = call(load_kernel, [PAIR], info, [mine])
    mixed, = call(functools.partial(blend_kernel, False), [PAIR], at_y, [mine, near_x])
    far_y = permute(mixed, GATHER[1])
    mixed, = call(functools.partial(blend_kernel, True), [PAIR], at_x, [other, near_y])
    far_x = permute(mixed, GATHER[0])
    second_slot = intensity[0, 1]
    shared = permute(second_slot, DIAGONAL)

    tabs = tables(here, tap_rows(fresnel_taps), fourier())
    patches, waves, spectrum = call(
        down_kernel, [ALL, ALL, FIELD], here,
        [mine, near_x, far_y, other, near_y, far_x, illumination, *tabs], WORK
    )
    grad_high, x_high, y_high, state = call(
        turn_up_kernel, [PAIR, FIELD, FIELD, STATE], here,
        [spectrum, intensity[0, 0], shared, waves, patches, *tabs], WORK
    )
    came_high = [permute(x_high, SCATTER[0]), permute(y_high, SCATTER[1])]
    grad_low, x_low, y_low = call(up_kernel, [PAIR, FIELD, FIELD], here, [state, waves, patches, *tabs], WORK)
    came_low = [permute(x_low, SCATTER[0]), permute(y_low, SCATTER[1])]
    parts = []
    for channel, there in ((0, at_x), (1, at_y)):
        straight, cross, stay, leaving = call(
            functools.partial(turn_kernel, channel), [FIELD] * 4, jnp.concatenate([here, there]),
            [grad_low, grad_high, came_low[channel], came_high[channel]]
        )
        way = 1 - channel
        parts += [stay, permute(leaving, SWAP), permute(straight, SCATTER[way]), permute(cross, CROSSED[way])]
    out, = call(final_kernel, [PAIR], here, parts)
    return out[:, :, None]


def solution(mesh):
    placed = (
        P("depth", None, "tiles", None, None),
        P(),
        P(),
        P("tiles", None, None, None),
        P("tiles", None, None),
        P("tiles"),
    )
    return jax.shard_map(
        step,
        mesh=mesh,
        in_specs=placed,
        out_specs=P("depth", None, "tiles", None, None),
        check_vma=False,
    )
```

```python
import functools
import math

import jax
import jax.numpy as jnp
from jax import lax
from jax.experimental import pallas as pl
from jax.experimental.pallas import tpu as pltpu
from jax.sharding import PartitionSpec as P

GX = 4
ROWS = 16
TILES = 64
N = 256
CH = 32
BF = jnp.bfloat16
F32 = jnp.float32
FIELD = jax.ShapeDtypeStruct((2, N, N), F32)
PAIR = jax.ShapeDtypeStruct((2, 2, N, N), F32)
ALL = jax.ShapeDtypeStruct((4, 2, N, N), F32)
VS = pl.BlockSpec(memory_space=pltpu.VMEM)
SS = pl.BlockSpec(memory_space=pltpu.SMEM)


def split(x):
    high = x.astype(BF)
    return high, (x - high.astype(F32)).astype(BF)


def dot3(left_high, left_low, right_high, right_low):
    dot = functools.partial(jnp.dot, preferred_element_type=F32)
    return dot(left_high, right_high) + dot(left_high, right_low) + dot(left_low, right_high)


def put_left(refs, index, re, im):
    for ref, r, m in zip(refs, split(re), split(im)):
        ref[index, 0:N, 0:N] = r
        ref[index, N : 2 * N, N : 2 * N] = r
        ref[index, N : 2 * N, 0:N] = m
        ref[index, 0:N, N : 2 * N] = -m


def put_right(refs, index, re, im):
    for ref, r, m in zip(refs, split(re), split(im)):
        ref[index, 0:N] = r
        ref[index, N : 2 * N] = m


def tables_kernel(spot, taps, dft, left_high, left_low, right_high, right_low, a_high, a_low, b_high, b_low):
    left = (left_high, left_low)
    right = (right_high, right_low)
    a = (a_high, a_low)
    b = (b_high, b_low)
    row = lax.broadcasted_iota(jnp.int32, (N, N), 0)
    col = lax.broadcasted_iota(jnp.int32, (N, N), 1)

    def circulant(k):
        base = jnp.broadcast_to(taps[k : k + 1, :], (N, N))
        return pltpu.roll(base, 0, 1, stride=1, stride_axis=0)

    rings = [circulant(0), circulant(1)]
    rings += [ring.T for ring in rings]
    fr, fi = dft[0], dft[1]

    def bands(shift):
        inside = jnp.abs(((row - shift) & (N - 1)) - ((col - shift) & (N - 1))) <= 15
        return [jnp.where(inside, ring, 0.0) for ring in rings]

    def multiply():
        m = dot3(a_high[0], a_low[0], b_high[0], b_low[0])
        return m[:N], m[N:]

    tr, ti, ttr, tti = bands(spot[0])
    put_left(left, 0, tr, ti)
    put_left(left, 1, ttr, -tti)
    put_left(a, 0, fr, fi)
    put_right(b, 0, tr, ti)
    mr, mi = multiply()
    put_left(left, 2, mr, mi)
    put_left(a, 0, ttr, tti)
    put_right(b, 0, fr, fi)
    mr, mi = multiply()
    put_left(left, 3, mr, -mi)
    tr, ti, ttr, tti = bands(spot[1])
    put_right(right, 0, ttr, tti)
    put_right(right, 1, tr, -ti)
    put_left(a, 0, ttr, tti)
    mr, mi = multiply()
    put_right(right, 2, mr, mi)
    put_left(a, 0, fr, fi)
    put_right(b, 0, tr, ti)
    mr, mi = multiply()
    put_right(right, 3, mr, -mi)


def tables(spot, taps, dft):
    return pl.pallas_call(
        tables_kernel,
        out_shape=[jax.ShapeDtypeStruct((4, 2 * N, 2 * N), BF)] * 2
        + [jax.ShapeDtypeStruct((4, 2 * N, N), BF)] * 2,
        in_specs=[SS, VS, VS],
        out_specs=[VS] * 4,
        scratch_shapes=[pltpu.VMEM((1, 2 * N, 2 * N), BF)] * 2 + [pltpu.VMEM((1, 2 * N, N), BF)] * 2,
        compiler_params=pltpu.CompilerParams(vmem_limit_bytes=12 << 20),
        name="tables",
    )(spot, taps, dft)


def tap_rows(taps):
    rows = jnp.pad(taps, ((0, 6), (0, N - taps.shape[1])))
    return jnp.roll(rows, -15, 1)


def chunks():
    return [(pl.ds(r0, CH), pl.ds(N + r0, CH), r0) for r0 in range(0, N, CH)]


def own_rows(spot, r0):
    row = lax.broadcasted_iota(jnp.int32, (CH, N), 0) + r0
    return ((row >= spot[0]).astype(jnp.int32) ^ spot[2]) == 1


def own_cols(spot):
    col = lax.broadcasted_iota(jnp.int32, (CH, N), 1)
    return ((col >= spot[1]).astype(jnp.int32) ^ spot[2]) == 1


WORK = (
    [pltpu.VMEM((2 * N, N), BF)] * 2
    + [pltpu.VMEM((2 * N, 2 * N), BF)] * 2
    + [pltpu.VMEM((2 * N, N), F32)]
)


def put_field(work, r0, re, im):
    for base, part in ((0, re), (N, im)):
        high, low = split(part)
        work[0][pl.ds(base + r0, CH)] = high
        work[1][pl.ds(base + r0, CH)] = low


def propagate(work, tabs, index):
    x_high, x_low, y_high, y_low, acc = work
    left_high, left_low, right_high, right_low = tabs
    half = N // 2
    spans = [(pl.ds(h * half, half), pl.ds(N + h * half, half)) for h in range(2)]
    for sl, s2 in spans:
        re = dot3(left_high[index, sl], left_low[index, sl], x_high[...], x_low[...])
        im = dot3(left_high[index, s2], left_low[index, s2], x_high[...], x_low[...])
        for ref, r, m in zip((y_high, y_low), split(re), split(im)):
            ref[sl, 0:N] = r
            ref[s2, N : 2 * N] = r
            ref[s2, 0:N] = m
            ref[sl, N : 2 * N] = -m
    for span in spans:
        for part in span:
            acc[part] = dot3(y_high[part], y_low[part], right_high[index], right_low[index])


def enter_slice(work, patch, wave):
    for sl, _, r0 in chunks():
        pr, pi, wr, wi = wave[0, sl], wave[1, sl], patch[0, sl], patch[1, sl]
        put_field(work, r0, pr * wr - pi * wi, pr * wi + pi * wr)


def leave(work, wave):
    acc = work[4]
    for sl, s2, _ in chunks():
        wave[0, sl] = acc[sl]
        wave[1, sl] = acc[s2]


def leave_slice(work, spot, patch, wave, grad, sent_x, sent_y, onward):
    acc = work[4]
    mine_cols = own_cols(spot)
    for sl, s2, r0 in chunks():
        mr, mi, pr, pi = acc[sl], acc[s2], wave[0, sl], wave[1, sl]
        re = pr * mr + pi * mi
        im = pr * mi - pi * mr
        grad[0, sl] = re
        grad[1, sl] = im
        sent_x[sl] = jnp.where(mine_cols, 0.0, re)
        sent_y[sl] = jnp.where(own_rows(spot, r0), 0.0, im)
        if onward:
            wr, wi = patch[0, sl], patch[1, sl]
            put_field(work, r0, wr * mr + wi * mi, wr * mi - wi * mr)


def down_kernel(spot, *refs):
    mine, near_x, far_y, other, near_y, far_x = refs[0:6]
    probe, tabs = refs[6], refs[7:11]
    patches, waves, spectrum = refs[11:14]
    work = refs[14:]
    core = spot[2]
    cols = own_cols(spot)
    for q in range(2):
        for sl, _, r0 in chunks():
            rows = own_rows(spot, r0)
            for c in range(2):
                inner = jnp.where(cols, mine[q, c, sl], near_x[q, c, sl])
                patches[2 * core + q, c, sl] = jnp.where(rows, inner, far_y[q, c, sl])
                inner = jnp.where(rows, other[q, c, sl], near_y[q, c, sl])
                patches[2 - 2 * core + q, c, sl] = jnp.where(cols, inner, far_x[q, c, sl])
    for c in range(2):
        waves[0, c] = pltpu.roll(pltpu.roll(probe[c], spot[0], 0), spot[1], 1)
    for k in range(4):
        enter_slice(work, patches.at[k], waves.at[k])
        propagate(work, tabs, 0 if k < 3 else 2)
        leave(work, waves.at[k + 1] if k < 3 else spectrum)


def save(work, state):
    state[0] = work[0][...]
    state[1] = work[1][...]


def turn_up_kernel(spot, *refs):
    spectrum, measured, shared, waves, patches, tabs = refs[0], refs[1], refs[2], refs[3], refs[4], refs[5:9]
    grad, sent_x, sent_y, state = refs[9:13]
    work = refs[13:]
    upper = spot[2] == 1
    scale = 2.0 * spot[3].astype(F32)
    for sl, _, r0 in chunks():
        sr, si = spectrum[0, sl], spectrum[1, sl]
        target = jnp.where(upper, shared[sl], measured[sl])
        misfit = (sr * sr + si * si - target) * scale
        put_field(work, r0, misfit * sr, misfit * si)
    for k in (3, 2):
        propagate(work, tabs, 3 if k == 3 else 1)
        leave_slice(work, spot, patches.at[k], waves.at[k], grad.at[k - 2], sent_x.at[k - 2], sent_y.at[k - 2], True)
    save(work, state)


def up_kernel(spot, *refs):
    state, waves, patches, tabs = refs[0], refs[1], refs[2], refs[3:7]
    grad, sent_x, sent_y = refs[7:10]
    work = refs[10:]
    work[0][...] = state[0]
    work[1][...] = state[1]
    for k in (1, 0):
        propagate(work, tabs, 1)
        leave_slice(work, spot, patches.at[k], waves.at[k], grad.at[k], sent_x.at[k], sent_y.at[k], k > 0)


STATE = jax.ShapeDtypeStruct((2, 2 * N, N), BF)


def call(kernel, outs, spot, args, scratch=(), where=VS):
    room = (12 if scratch else 6) << 20
    return pl.pallas_call(
        kernel,
        out_shape=outs,
        in_specs=[SS] + [VS] * len(args),
        out_specs=[where] * len(outs),
        scratch_shapes=list(scratch),
        compiler_params=pltpu.CompilerParams(vmem_limit_bytes=room),
    )(spot, *args)


def load_kernel(spot, block, out):
    for q in range(2):
        for c in range(2):
            for sl, _, _ in chunks():
                out[q, c, sl] = block[q, c, sl]


def blend_kernel(by_rows, spot, own, near, mixed):
    cols = own_cols(spot)
    for sl, _, r0 in chunks():
        mask = own_rows(spot, r0) if by_rows else cols
        for q in range(2):
            for c in range(2):
                mixed[q, c, sl] = jnp.where(mask, own[q, c, sl], near[q, c, sl])


def turn_kernel(channel, spots, *refs):
    grads, came, outs = refs[0:2], refs[2:4], refs[4:8]
    here = [spots[i] for i in range(3)]
    there = [spots[4 + i] for i in range(3)]
    cols, there_cols = own_cols(here), own_cols(there)
    upper = spots[2] == 1
    for sl, _, r0 in chunks():
        rows = own_rows(here, r0)
        if channel == 1:
            first, second, mask = rows, cols, there_cols
        else:
            first, second, mask = cols, rows, own_rows(there, r0)
        for q in range(2):
            sent, kept = [], []
            for grad, block in zip(grads, came):
                g = jnp.where(first, grad[q, channel, sl], 0.0)
                v = block[q, sl]
                sent.append(jnp.where(second, 0.0, g) + jnp.where(mask, 0.0, v))
                kept.append(jnp.where(second, g, 0.0) + jnp.where(mask, v, 0.0))
            outs[0][q, sl] = jnp.where(upper, sent[1], sent[0])
            outs[1][q, sl] = jnp.where(upper, sent[0], sent[1])
            outs[2][q, sl] = jnp.where(upper, kept[1], kept[0])
            outs[3][q, sl] = jnp.where(upper, kept[0], kept[1])


def final_kernel(spot, *refs):
    out, buffer, done = refs[8], refs[9], refs[10]
    copies = []
    for q in range(2):
        for c in range(2):
            for sl, _, _ in chunks():
                a, b, x, y = (refs[4 * c + i][q, sl] for i in range(4))
                buffer[q, c, sl] = (a + b) + (x + y)
            copies.append(pltpu.make_async_copy(buffer.at[q, c], out.at[q, c], done.at[2 * q + c]))
            copies[-1].start()
    for copy in copies:
        copy.wait()


def moved(t, dx, dy):
    return ((t // GX + dy) % ROWS) * GX + (t % GX + dx) % GX


def pairs_of(*per_core):
    out = []
    for d, step in enumerate(per_core):
        if step is not None:
            out += [(d * TILES + t, d * TILES + moved(t, *step)) for t in range(TILES)]
    return out


GATHER = (pairs_of((-1, 0), (1, 0)), pairs_of((0, -1), (0, 1)))
SCATTER = (pairs_of((1, 0), (-1, 0)), pairs_of((0, 1), (0, -1)))
INFO = (pairs_of((1, 0), (1, 0)), pairs_of((0, 1), (0, 1)))
CROSSED = [[(a, (b + TILES) % (2 * TILES)) for a, b in way] for way in SCATTER]
DIAGONAL = pairs_of(None, (1, 1))
SWAP = [(d * TILES + t, (1 - d) * TILES + t) for d in range(2) for t in range(TILES)]


def permute(block, pairs):
    return lax.ppermute(block, ("depth", "tiles"), pairs)


def fourier():
    row = lax.broadcasted_iota(jnp.int32, (N, N), 0)
    col = lax.broadcasted_iota(jnp.int32, (N, N), 1)
    phase = (row * col % N).astype(F32) * (2.0 * math.pi / N)
    scale = 1.0 / math.sqrt(N)
    return jnp.stack([jnp.cos(phase) * scale, -jnp.sin(phase) * scale])


def step(transmission, illumination, fresnel_taps, intensity, offsets, counts):
    core = lax.axis_index("depth").astype(jnp.int32)
    mine = transmission[:, :, 0]
    other = permute(mine, SWAP)
    near_x = permute(mine, GATHER[0])
    alive = (core < counts[0]).astype(jnp.int32)
    info = jnp.concatenate([jnp.where(core == 0, offsets[0, 0], offsets[0, 1]), core[None], alive[None]])
    left = permute(info, INFO[0])
    up = permute(info, INFO[1])
    upleft = permute(info, DIAGONAL)
    here = jnp.where(core == 0, info, upleft)
    at_y = jnp.where(core == 0, up, left)
    at_x = jnp.where(core == 0, left, up)
    near_y = permute(other, GATHER[1])

    mine, = call(load_kernel, [PAIR], info, [mine])
    mixed, = call(functools.partial(blend_kernel, False), [PAIR], at_y, [mine, near_x])
    far_y = permute(mixed, GATHER[1])
    mixed, = call(functools.partial(blend_kernel, True), [PAIR], at_x, [other, near_y])
    far_x = permute(mixed, GATHER[0])
    second_slot = intensity[0, 1]
    shared = permute(second_slot, DIAGONAL)

    tabs = tables(here, tap_rows(fresnel_taps), fourier())
    patches, waves, spectrum = call(
        down_kernel, [ALL, ALL, FIELD], here,
        [mine, near_x, far_y, other, near_y, far_x, illumination, *tabs], WORK
    )
    grad_high, x_high, y_high, state = call(
        turn_up_kernel, [PAIR, FIELD, FIELD, STATE], here,
        [spectrum, intensity[0, 0], shared, waves, patches, *tabs], WORK
    )
    came_high = [permute(x_high, SCATTER[0]), permute(y_high, SCATTER[1])]
    grad_low, x_low, y_low = call(up_kernel, [PAIR, FIELD, FIELD], here, [state, waves, patches, *tabs], WORK)
    came_low = [permute(x_low, SCATTER[0]), permute(y_low, SCATTER[1])]
    parts = []
    for channel, there in ((0, at_x), (1, at_y)):
        straight, cross, stay, leaving = call(
            functools.partial(turn_kernel, channel), [FIELD] * 4, jnp.concatenate([here, there]),
            [grad_low, grad_high, came_low[channel], came_high[channel]]
        )
        way = 1 - channel
        parts += [stay, permute(leaving, SWAP), permute(straight, SCATTER[way]), permute(cross, CROSSED[way])]
    scratch = [pltpu.VMEM((2, 2, N, N), F32), pltpu.SemaphoreType.DMA((4,))]
    out, = call(final_kernel, [PAIR], here, parts, scratch, pl.BlockSpec(memory_space=pl.ANY))
    return out[:, :, None]


def solution(mesh):
    placed = (
        P("depth", None, "tiles", None, None),
        P(),
        P(),
        P("tiles", None, None, None),
        P("tiles", None, None),
        P("tiles"),
    )
    return jax.shard_map(
        step,
        mesh=mesh,
        in_specs=placed,
        out_specs=P("depth", None, "tiles", None, None),
        check_vma=False,
    )
```

```python
import functools
import math

import jax
import jax.numpy as jnp
from jax import lax
from jax.experimental import pallas as pl
from jax.experimental.pallas import tpu as pltpu
from jax.sharding import PartitionSpec as P

GX = 4
ROWS = 16
TILES = 64
N = 256
CH = 32
BF = jnp.bfloat16
F32 = jnp.float32
FIELD = jax.ShapeDtypeStruct((2, N, N), F32)
PAIR = jax.ShapeDtypeStruct((2, 2, N, N), F32)
ALL = jax.ShapeDtypeStruct((4, 2, N, N), F32)
VS = pl.BlockSpec(memory_space=pltpu.VMEM)
SS = pl.BlockSpec(memory_space=pltpu.SMEM)


def split(x):
    high = x.astype(BF)
    return high, (x - high.astype(F32)).astype(BF)


def dot3(left_high, left_low, right_high, right_low):
    dot = functools.partial(jnp.dot, preferred_element_type=F32)
    return dot(left_high, right_high) + dot(left_high, right_low) + dot(left_low, right_high)


def put_left(refs, index, re, im):
    for ref, r, m in zip(refs, split(re), split(im)):
        ref[index, 0:N, 0:N] = r
        ref[index, N : 2 * N, N : 2 * N] = r
        ref[index, N : 2 * N, 0:N] = m
        ref[index, 0:N, N : 2 * N] = -m


def put_right(refs, index, re, im):
    for ref, r, m in zip(refs, split(re), split(im)):
        ref[index, 0:N] = r
        ref[index, N : 2 * N] = m


def tables_kernel(spot, taps, dft, left_high, left_low, right_high, right_low, a_high, a_low, b_high, b_low):
    left = (left_high, left_low)
    right = (right_high, right_low)
    a = (a_high, a_low)
    b = (b_high, b_low)
    row = lax.broadcasted_iota(jnp.int32, (N, N), 0)
    col = lax.broadcasted_iota(jnp.int32, (N, N), 1)

    def circulant(k):
        base = jnp.broadcast_to(taps[k : k + 1, :], (N, N))
        return pltpu.roll(base, 0, 1, stride=1, stride_axis=0)

    rings = [circulant(0), circulant(1)]
    rings += [ring.T for ring in rings]
    fr, fi = dft[0], dft[1]

    def bands(shift):
        inside = jnp.abs(((row - shift) & (N - 1)) - ((col - shift) & (N - 1))) <= 15
        return [jnp.where(inside, ring, 0.0) for ring in rings]

    def multiply():
        m = dot3(a_high[0], a_low[0], b_high[0], b_low[0])
        return m[:N], m[N:]

    tr, ti, ttr, tti = bands(spot[0])
    put_left(left, 0, tr, ti)
    put_left(left, 1, ttr, -tti)
    put_left(a, 0, fr, fi)
    put_right(b, 0, tr, ti)
    mr, mi = multiply()
    put_left(left, 2, mr, mi)
    put_left(a, 0, ttr, tti)
    put_right(b, 0, fr, fi)
    mr, mi = multiply()
    put_left(left, 3, mr, -mi)
    tr, ti, ttr, tti = bands(spot[1])
    put_right(right, 0, ttr, tti)
    put_right(right, 1, tr, -ti)
    put_left(a, 0, ttr, tti)
    mr, mi = multiply()
    put_right(right, 2, mr, mi)
    put_left(a, 0, fr, fi)
    put_right(b, 0, tr, ti)
    mr, mi = multiply()
    put_right(right, 3, mr, -mi)


def tables(spot, taps, dft):
    return pl.pallas_call(
        tables_kernel,
        out_shape=[jax.ShapeDtypeStruct((4, 2 * N, 2 * N), BF)] * 2
        + [jax.ShapeDtypeStruct((4, 2 * N, N), BF)] * 2,
        in_specs=[SS, VS, VS],
        out_specs=[VS] * 4,
        scratch_shapes=[pltpu.VMEM((1, 2 * N, 2 * N), BF)] * 2 + [pltpu.VMEM((1, 2 * N, N), BF)] * 2,
        compiler_params=pltpu.CompilerParams(vmem_limit_bytes=12 << 20),
        name="tables",
    )(spot, taps, dft)


def tap_rows(taps):
    rows = jnp.pad(taps, ((0, 6), (0, N - taps.shape[1])))
    return jnp.roll(rows, -15, 1)


def chunks():
    return [(pl.ds(r0, CH), pl.ds(N + r0, CH), r0) for r0 in range(0, N, CH)]


def own_rows(spot, r0):
    row = lax.broadcasted_iota(jnp.int32, (CH, N), 0) + r0
    return ((row >= spot[0]).astype(jnp.int32) ^ spot[2]) == 1


def own_cols(spot):
    col = lax.broadcasted_iota(jnp.int32, (CH, N), 1)
    return ((col >= spot[1]).astype(jnp.int32) ^ spot[2]) == 1


WORK = (
    [pltpu.VMEM((2 * N, N), BF)] * 2
    + [pltpu.VMEM((2 * N, 2 * N), BF)] * 2
    + [pltpu.VMEM((2 * N, N), F32)]
)


def put_field(work, r0, re, im):
    for base, part in ((0, re), (N, im)):
        high, low = split(part)
        work[0][pl.ds(base + r0, CH)] = high
        work[1][pl.ds(base + r0, CH)] = low


def propagate(work, tabs, index):
    x_high, x_low, y_high, y_low, acc = work
    left_high, left_low, right_high, right_low = tabs
    half = N // 2
    spans = [(pl.ds(h * half, half), pl.ds(N + h * half, half)) for h in range(2)]
    for sl, s2 in spans:
        re = dot3(left_high[index, sl], left_low[index, sl], x_high[...], x_low[...])
        im = dot3(left_high[index, s2], left_low[index, s2], x_high[...], x_low[...])
        for ref, r, m in zip((y_high, y_low), split(re), split(im)):
            ref[sl, 0:N] = r
            ref[s2, N : 2 * N] = r
            ref[s2, 0:N] = m
            ref[sl, N : 2 * N] = -m
    for span in spans:
        for part in span:
            acc[part] = dot3(y_high[part], y_low[part], right_high[index], right_low[index])


def enter_slice(work, patch, wave):
    for sl, _, r0 in chunks():
        pr, pi, wr, wi = wave[0, sl], wave[1, sl], patch[0, sl], patch[1, sl]
        put_field(work, r0, pr * wr - pi * wi, pr * wi + pi * wr)


def leave(work, wave):
    acc = work[4]
    for sl, s2, _ in chunks():
        wave[0, sl] = acc[sl]
        wave[1, sl] = acc[s2]


def leave_slice(work, spot, patch, wave, grad, sent_x, sent_y, onward):
    acc = work[4]
    mine_cols = own_cols(spot)
    for sl, s2, r0 in chunks():
        mr, mi, pr, pi = acc[sl], acc[s2], wave[0, sl], wave[1, sl]
        re = pr * mr + pi * mi
        im = pr * mi - pi * mr
        grad[0, sl] = re
        grad[1, sl] = im
        sent_x[sl] = jnp.where(mine_cols, 0.0, re)
        sent_y[sl] = jnp.where(own_rows(spot, r0), 0.0, im)
        if onward:
            wr, wi = patch[0, sl], patch[1, sl]
            put_field(work, r0, wr * mr + wi * mi, wr * mi - wi * mr)


def down_kernel(spot, *refs):
    mine, near_x, far_y, other, near_y, far_x = refs[0:6]
    probe, tabs = refs[6], refs[7:11]
    patches, waves, spectrum = refs[11:14]
    work = refs[14:]
    core = spot[2]
    cols = own_cols(spot)
    for q in range(2):
        for sl, _, r0 in chunks():
            rows = own_rows(spot, r0)
            for c in range(2):
                inner = jnp.where(cols, mine[q, c, sl], near_x[q, c, sl])
                patches[2 * core + q, c, sl] = jnp.where(rows, inner, far_y[q, c, sl])
                inner = jnp.where(rows, other[q, c, sl], near_y[q, c, sl])
                patches[2 - 2 * core + q, c, sl] = jnp.where(cols, inner, far_x[q, c, sl])
    for c in range(2):
        waves[0, c] = pltpu.roll(pltpu.roll(probe[c], spot[0], 0), spot[1], 1)
    for k in range(4):
        enter_slice(work, patches.at[k], waves.at[k])
        propagate(work, tabs, 0 if k < 3 else 2)
        leave(work, waves.at[k + 1] if k < 3 else spectrum)


def save(work, state):
    state[0] = work[0][...]
    state[1] = work[1][...]


def turn_up_kernel(spot, *refs):
    spectrum, measured, shared, waves, patches, tabs = refs[0], refs[1], refs[2], refs[3], refs[4], refs[5:9]
    grad, sent_x, sent_y, state = refs[9:13]
    work = refs[13:]
    upper = spot[2] == 1
    scale = 2.0 * spot[3].astype(F32)
    for sl, _, r0 in chunks():
        sr, si = spectrum[0, sl], spectrum[1, sl]
        target = jnp.where(upper, shared[sl], measured[sl])
        misfit = (sr * sr + si * si - target) * scale
        put_field(work, r0, misfit * sr, misfit * si)
    for k in (3, 2):
        propagate(work, tabs, 3 if k == 3 else 1)
        leave_slice(work, spot, patches.at[k], waves.at[k], grad.at[k - 2], sent_x.at[k - 2], sent_y.at[k - 2], True)
    save(work, state)


def up_kernel(k, spot, *refs):
    state, waves, patches, tabs = refs[0], refs[1], refs[2], refs[3:7]
    grad, sent_x, sent_y = refs[7:10]
    work = refs[11:] if k > 0 else refs[10:]
    work[0][...] = state[0]
    work[1][...] = state[1]
    propagate(work, tabs, 1)
    leave_slice(work, spot, patches.at[k], waves.at[k], grad, sent_x, sent_y, k > 0)
    if k > 0:
        save(work, refs[10])


PLANE = jax.ShapeDtypeStruct((N, N), F32)
STATE = jax.ShapeDtypeStruct((2, 2 * N, N), BF)


def call(kernel, outs, spot, args, scratch=(), where=VS):
    room = (12 if scratch else 6) << 20
    return pl.pallas_call(
        kernel,
        out_shape=outs,
        in_specs=[SS] + [VS] * len(args),
        out_specs=[where] * len(outs),
        scratch_shapes=list(scratch),
        compiler_params=pltpu.CompilerParams(vmem_limit_bytes=room),
    )(spot, *args)


def load_kernel(spot, block, out):
    for q in range(2):
        for c in range(2):
            for sl, _, _ in chunks():
                out[q, c, sl] = block[q, c, sl]


def blend_kernel(by_rows, spot, own, near, mixed):
    cols = own_cols(spot)
    for sl, _, r0 in chunks():
        mask = own_rows(spot, r0) if by_rows else cols
        for q in range(2):
            for c in range(2):
                mixed[q, c, sl] = jnp.where(mask, own[q, c, sl], near[q, c, sl])


def turn_kernel(channel, spots, *refs):
    low, high, came_low, came_high, outs = refs[0:2], refs[2], refs[3:5], refs[5], refs[6:10]
    here = [spots[i] for i in range(3)]
    there = [spots[4 + i] for i in range(3)]
    cols, there_cols = own_cols(here), own_cols(there)
    upper = spots[2] == 1
    for sl, _, r0 in chunks():
        rows = own_rows(here, r0)
        if channel == 1:
            first, second, mask = rows, cols, there_cols
        else:
            first, second, mask = cols, rows, own_rows(there, r0)
        for q in range(2):
            sent, kept = [], []
            for grad, v in ((low[q][channel, sl], came_low[q][sl]), (high[q, channel, sl], came_high[q, sl])):
                g = jnp.where(first, grad, 0.0)
                sent.append(jnp.where(second, 0.0, g) + jnp.where(mask, 0.0, v))
                kept.append(jnp.where(second, g, 0.0) + jnp.where(mask, v, 0.0))
            outs[0][q, sl] = jnp.where(upper, sent[1], sent[0])
            outs[1][q, sl] = jnp.where(upper, sent[0], sent[1])
            outs[2][q, sl] = jnp.where(upper, kept[1], kept[0])
            outs[3][q, sl] = jnp.where(upper, kept[0], kept[1])


def presum_kernel(spot, *refs):
    for c in range(2):
        for q in range(2):
            for sl, _, _ in chunks():
                a, b, x = (refs[3 * c + i][q, sl] for i in range(3))
                refs[6 + c][q, sl] = (a + b) + x


def final_kernel(spot, *refs):
    out, buffer, done = refs[4], refs[5], refs[6]
    copies = []
    for q in range(2):
        for c in range(2):
            for sl, _, _ in chunks():
                buffer[q, c, sl] = refs[c][q, sl] + refs[2 + c][q, sl]
            copies.append(pltpu.make_async_copy(buffer.at[q, c], out.at[q, c], done.at[2 * q + c]))
            copies[-1].start()
    for copy in copies:
        copy.wait()


def moved(t, dx, dy):
    return ((t // GX + dy) % ROWS) * GX + (t % GX + dx) % GX


def pairs_of(*per_core):
    out = []
    for d, step in enumerate(per_core):
        if step is not None:
            out += [(d * TILES + t, d * TILES + moved(t, *step)) for t in range(TILES)]
    return out


GATHER = (pairs_of((-1, 0), (1, 0)), pairs_of((0, -1), (0, 1)))
SCATTER = (pairs_of((1, 0), (-1, 0)), pairs_of((0, 1), (0, -1)))
INFO = (pairs_of((1, 0), (1, 0)), pairs_of((0, 1), (0, 1)))
CROSSED = [[(a, (b + TILES) % (2 * TILES)) for a, b in way] for way in SCATTER]
DIAGONAL = pairs_of(None, (1, 1))
SWAP = [(d * TILES + t, (1 - d) * TILES + t) for d in range(2) for t in range(TILES)]


def permute(block, pairs):
    return lax.ppermute(block, ("depth", "tiles"), pairs)


def fourier():
    row = lax.broadcasted_iota(jnp.int32, (N, N), 0)
    col = lax.broadcasted_iota(jnp.int32, (N, N), 1)
    phase = (row * col % N).astype(F32) * (2.0 * math.pi / N)
    scale = 1.0 / math.sqrt(N)
    return jnp.stack([jnp.cos(phase) * scale, -jnp.sin(phase) * scale])


def step(transmission, illumination, fresnel_taps, intensity, offsets, counts):
    core = lax.axis_index("depth").astype(jnp.int32)
    mine = transmission[:, :, 0]
    other = permute(mine, SWAP)
    near_x = permute(mine, GATHER[0])
    alive = (core < counts[0]).astype(jnp.int32)
    info = jnp.concatenate([jnp.where(core == 0, offsets[0, 0], offsets[0, 1]), core[None], alive[None]])
    left = permute(info, INFO[0])
    up = permute(info, INFO[1])
    upleft = permute(info, DIAGONAL)
    here = jnp.where(core == 0, info, upleft)
    at_y = jnp.where(core == 0, up, left)
    at_x = jnp.where(core == 0, left, up)
    near_y = permute(other, GATHER[1])

    mine, = call(load_kernel, [PAIR], info, [mine])
    mixed, = call(functools.partial(blend_kernel, False), [PAIR], at_y, [mine, near_x])
    far_y = permute(mixed, GATHER[1])
    mixed, = call(functools.partial(blend_kernel, True), [PAIR], at_x, [other, near_y])
    far_x = permute(mixed, GATHER[0])
    second_slot = intensity[0, 1]
    shared = permute(second_slot, DIAGONAL)

    tabs = tables(here, tap_rows(fresnel_taps), fourier())
    patches, waves, spectrum = call(
        down_kernel, [ALL, ALL, FIELD], here,
        [mine, near_x, far_y, other, near_y, far_x, illumination, *tabs], WORK
    )
    grad_high, x_high, y_high, state = call(
        turn_up_kernel, [PAIR, FIELD, FIELD, STATE], here,
        [spectrum, intensity[0, 0], shared, waves, patches, *tabs], WORK
    )
    came_high = [permute(x_high, SCATTER[0]), permute(y_high, SCATTER[1])]
    grad_low, came_low = [None, None], [None, None]
    for k in (1, 0):
        outs = call(
            functools.partial(up_kernel, k), [FIELD, PLANE, PLANE] + [STATE] * k, here,
            [state, waves, patches, *tabs], WORK
        )
        grad_low[k] = outs[0]
        came_low[k] = [permute(outs[1], SCATTER[0]), permute(outs[2], SCATTER[1])]
        state = outs[3] if k else None
    parts, crosses = [], []
    for channel, there in ((0, at_x), (1, at_y)):
        straight, cross, stay, leaving = call(
            functools.partial(turn_kernel, channel), [FIELD] * 4, jnp.concatenate([here, there]),
            [*grad_low, grad_high, came_low[0][channel], came_low[1][channel], came_high[channel]]
        )
        way = 1 - channel
        parts += [stay, permute(leaving, SWAP), permute(straight, SCATTER[way])]
        crosses.append(permute(cross, CROSSED[way]))
    sums = call(presum_kernel, [FIELD] * 2, here, parts)
    scratch = [pltpu.VMEM((2, 2, N, N), F32), pltpu.SemaphoreType.DMA((4,))]
    out, = call(final_kernel, [PAIR], here, [*sums, *crosses], scratch, pl.BlockSpec(memory_space=pl.ANY))
    return out[:, :, None]


def solution(mesh):
    placed = (
        P("depth", None, "tiles", None, None),
        P(),
        P(),
        P("tiles", None, None, None),
        P("tiles", None, None),
        P("tiles"),
    )
    return jax.shard_map(
        step,
        mesh=mesh,
        in_specs=placed,
        out_specs=P("depth", None, "tiles", None, None),
        check_vma=False,
    )
```

```python
import functools
import math

import jax
import jax.numpy as jnp
from jax import lax
from jax.experimental import pallas as pl
from jax.experimental.pallas import tpu as pltpu
from jax.sharding import PartitionSpec as P

GX = 4
ROWS = 16
TILES = 64
N = 256
CH = 32
BF = jnp.bfloat16
F32 = jnp.float32
FIELD = jax.ShapeDtypeStruct((2, N, N), F32)
PAIR = jax.ShapeDtypeStruct((2, 2, N, N), F32)
VS = pl.BlockSpec(memory_space=pltpu.VMEM)
SS = pl.BlockSpec(memory_space=pltpu.SMEM)


def split(x):
    high = x.astype(BF)
    return high, (x - high.astype(F32)).astype(BF)


def dot3(left_high, left_low, right_high, right_low):
    dot = functools.partial(jnp.dot, preferred_element_type=F32)
    return dot(left_high, right_high) + dot(left_high, right_low) + dot(left_low, right_high)


def put_left(refs, index, re, im):
    for ref, r, m in zip(refs, split(re), split(im)):
        ref[index, 0:N, 0:N] = r
        ref[index, N : 2 * N, N : 2 * N] = r
        ref[index, N : 2 * N, 0:N] = m
        ref[index, 0:N, N : 2 * N] = -m


def put_right(refs, index, re, im):
    for ref, r, m in zip(refs, split(re), split(im)):
        ref[index, 0:N] = r
        ref[index, N : 2 * N] = m


def tables_kernel(spot, taps, dft, left_high, left_low, right_high, right_low, a_high, a_low, b_high, b_low):
    left = (left_high, left_low)
    right = (right_high, right_low)
    a = (a_high, a_low)
    b = (b_high, b_low)
    row = lax.broadcasted_iota(jnp.int32, (N, N), 0)
    col = lax.broadcasted_iota(jnp.int32, (N, N), 1)

    def circulant(k):
        base = jnp.broadcast_to(taps[k : k + 1, :], (N, N))
        return pltpu.roll(base, 0, 1, stride=1, stride_axis=0)

    rings = [circulant(0), circulant(1)]
    rings += [ring.T for ring in rings]
    fr, fi = dft[0], dft[1]

    def bands(shift):
        inside = jnp.abs(((row - shift) & (N - 1)) - ((col - shift) & (N - 1))) <= 15
        return [jnp.where(inside, ring, 0.0) for ring in rings]

    def multiply():
        m = dot3(a_high[0], a_low[0], b_high[0], b_low[0])
        return m[:N], m[N:]

    tr, ti, ttr, tti = bands(spot[0])
    put_left(left, 0, tr, ti)
    put_left(left, 1, ttr, -tti)
    put_left(a, 0, fr, fi)
    put_right(b, 0, tr, ti)
    mr, mi = multiply()
    put_left(left, 2, mr, mi)
    put_left(a, 0, ttr, tti)
    put_right(b, 0, fr, fi)
    mr, mi = multiply()
    put_left(left, 3, mr, -mi)
    tr, ti, ttr, tti = bands(spot[1])
    put_right(right, 0, ttr, tti)
    put_right(right, 1, tr, -ti)
    put_left(a, 0, ttr, tti)
    mr, mi = multiply()
    put_right(right, 2, mr, mi)
    put_left(a, 0, fr, fi)
    put_right(b, 0, tr, ti)
    mr, mi = multiply()
    put_right(right, 3, mr, -mi)


def tables(spot, taps, dft):
    return pl.pallas_call(
        tables_kernel,
        out_shape=[jax.ShapeDtypeStruct((4, 2 * N, 2 * N), BF)] * 2
        + [jax.ShapeDtypeStruct((4, 2 * N, N), BF)] * 2,
        in_specs=[SS, VS, VS],
        out_specs=[VS] * 4,
        scratch_shapes=[pltpu.VMEM((1, 2 * N, 2 * N), BF)] * 2 + [pltpu.VMEM((1, 2 * N, N), BF)] * 2,
        compiler_params=pltpu.CompilerParams(vmem_limit_bytes=12 << 20),
        name="tables",
    )(spot, taps, dft)


def tap_rows(taps):
    rows = jnp.pad(taps, ((0, 6), (0, N - taps.shape[1])))
    return jnp.roll(rows, -15, 1)


def chunks():
    return [(pl.ds(r0, CH), pl.ds(N + r0, CH), r0) for r0 in range(0, N, CH)]


def own_rows(spot, r0):
    row = lax.broadcasted_iota(jnp.int32, (CH, N), 0) + r0
    return ((row >= spot[0]).astype(jnp.int32) ^ spot[2]) == 1


def own_cols(spot):
    col = lax.broadcasted_iota(jnp.int32, (CH, N), 1)
    return ((col >= spot[1]).astype(jnp.int32) ^ spot[2]) == 1


WORK = (
    [pltpu.VMEM((2 * N, N), BF)] * 2
    + [pltpu.VMEM((2 * N, 2 * N), BF)] * 2
    + [pltpu.VMEM((2 * N, N), F32)]
)


def put_field(work, r0, re, im):
    for base, part in ((0, re), (N, im)):
        high, low = split(part)
        work[0][pl.ds(base + r0, CH)] = high
        work[1][pl.ds(base + r0, CH)] = low


def propagate(work, tabs, index):
    x_high, x_low, y_high, y_low, acc = work
    left_high, left_low, right_high, right_low = tabs
    half = N // 2
    spans = [(pl.ds(h * half, half), pl.ds(N + h * half, half)) for h in range(2)]
    for sl, s2 in spans:
        re = dot3(left_high[index, sl], left_low[index, sl], x_high[...], x_low[...])
        im = dot3(left_high[index, s2], left_low[index, s2], x_high[...], x_low[...])
        for ref, r, m in zip((y_high, y_low), split(re), split(im)):
            ref[sl, 0:N] = r
            ref[s2, N : 2 * N] = r
            ref[s2, 0:N] = m
            ref[sl, N : 2 * N] = -m
    for span in spans:
        for part in span:
            acc[part] = dot3(y_high[part], y_low[part], right_high[index], right_low[index])


def enter_slice(work, patch, wave):
    for sl, _, r0 in chunks():
        pr, pi, wr, wi = wave[0, sl], wave[1, sl], patch[0, sl], patch[1, sl]
        put_field(work, r0, pr * wr - pi * wi, pr * wi + pi * wr)


def leave(work, wave):
    acc = work[4]
    for sl, s2, _ in chunks():
        wave[0, sl] = acc[sl]
        wave[1, sl] = acc[s2]


def leave_slice(work, spot, patch, wave, grad, sent_x, sent_y, onward):
    acc = work[4]
    mine_cols = own_cols(spot)
    for sl, s2, r0 in chunks():
        mr, mi, pr, pi = acc[sl], acc[s2], wave[0, sl], wave[1, sl]
        re = pr * mr + pi * mi
        im = pr * mi - pi * mr
        grad[0, sl] = re
        grad[1, sl] = im
        sent_x[sl] = jnp.where(mine_cols, 0.0, re)
        sent_y[sl] = jnp.where(own_rows(spot, r0), 0.0, im)
        if onward:
            wr, wi = patch[0, sl], patch[1, sl]
            put_field(work, r0, wr * mr + wi * mi, wr * mi - wi * mr)


def gather_patch(spot, p, own, near, far, out):
    cols = own_cols(spot)
    for sl, _, r0 in chunks():
        rows = own_rows(spot, r0)
        inner, outer = (cols, rows) if p % 2 == 0 else (rows, cols)
        for c in range(2):
            out[c, sl] = jnp.where(outer, jnp.where(inner, own[c, sl], near[c, sl]), far[c, sl])


def first_kernel(spot, *refs):
    own, near, far, probe, tabs = refs[0:2], refs[2:4], refs[4:6], refs[6], refs[7:11]
    patches, waves, work = refs[11:13], refs[13:16], refs[16:]
    for c in range(2):
        waves[0][c] = pltpu.roll(pltpu.roll(probe[c], spot[0], 0), spot[1], 1)
    for p in range(2):
        gather_patch(spot, p, own[p], near[p], far[p], patches[p])
        enter_slice(work, patches[p], waves[p])
        propagate(work, tabs, 0)
        leave(work, waves[p + 1])


def second_kernel(spot, *refs):
    own, near, far, wave, tabs = refs[0:2], refs[2:4], refs[4:6], refs[6], refs[7:11]
    patches, middle, spectrum, work = refs[11:13], refs[13], refs[14], refs[15:]
    for p in range(2):
        gather_patch(spot, p, own[p], near[p], far[p], patches[p])
        enter_slice(work, patches[p], middle if p else wave)
        propagate(work, tabs, 2 * p)
        leave(work, spectrum if p else middle)


def save(work, state):
    state[0] = work[0][...]
    state[1] = work[1][...]


def turn_up_kernel(spot, *refs):
    spectrum, measured, shared, waves, patches, tabs = refs[0], refs[1], refs[2], refs[3:5], refs[5:7], refs[7:11]
    grad, sent_x, sent_y, state = refs[11:15]
    work = refs[15:]
    upper = spot[2] == 1
    scale = 2.0 * spot[3].astype(F32)
    for sl, _, r0 in chunks():
        sr, si = spectrum[0, sl], spectrum[1, sl]
        target = jnp.where(upper, shared[sl], measured[sl])
        misfit = (sr * sr + si * si - target) * scale
        put_field(work, r0, misfit * sr, misfit * si)
    for k in (3, 2):
        propagate(work, tabs, 3 if k == 3 else 1)
        leave_slice(work, spot, patches[k - 2], waves[k - 2], grad.at[k - 2], sent_x.at[k - 2], sent_y.at[k - 2], True)
    save(work, state)


def up_kernel(k, spot, *refs):
    state, wave, patch, tabs = refs[0], refs[1], refs[2], refs[3:7]
    grad, sent_x, sent_y = refs[7:10]
    work = refs[11:] if k > 0 else refs[10:]
    work[0][...] = state[0]
    work[1][...] = state[1]
    propagate(work, tabs, 1)
    leave_slice(work, spot, patch, wave, grad, sent_x, sent_y, k > 0)
    if k > 0:
        save(work, refs[10])


PLANE = jax.ShapeDtypeStruct((N, N), F32)
STATE = jax.ShapeDtypeStruct((2, 2 * N, N), BF)


def call(kernel, outs, spot, args, scratch=(), where=VS):
    room = (12 if scratch else 6) << 20
    return pl.pallas_call(
        kernel,
        out_shape=outs,
        in_specs=[SS] + [VS] * len(args),
        out_specs=[where] * len(outs),
        scratch_shapes=list(scratch),
        compiler_params=pltpu.CompilerParams(vmem_limit_bytes=room),
    )(spot, *args)


def order_kernel(spot, mine, other, *outs):
    upper = spot[2] == 1
    for k in range(4):
        for c in range(2):
            for sl, _, _ in chunks():
                a, b = mine[k % 2, c, sl], other[k % 2, c, sl]
                outs[k][c, sl] = jnp.where(upper, b, a) if k < 2 else jnp.where(upper, a, b)


def blend_kernel(by_rows, spot, own, near, mixed):
    cols = own_cols(spot)
    for sl, _, r0 in chunks():
        mask = own_rows(spot, r0) if by_rows else cols
        for c in range(2):
            mixed[c, sl] = jnp.where(mask, own[c, sl], near[c, sl])


def turn_kernel(channel, spots, *refs):
    low, high, came_low, came_high, outs = refs[0:2], refs[2], refs[3:5], refs[5], refs[6:10]
    here = [spots[i] for i in range(3)]
    there = [spots[4 + i] for i in range(3)]
    cols, there_cols = own_cols(here), own_cols(there)
    upper = spots[2] == 1
    for sl, _, r0 in chunks():
        rows = own_rows(here, r0)
        if channel == 1:
            first, second, mask = rows, cols, there_cols
        else:
            first, second, mask = cols, rows, own_rows(there, r0)
        for q in range(2):
            sent, kept = [], []
            for grad, v in ((low[q][channel, sl], came_low[q][sl]), (high[q, channel, sl], came_high[q, sl])):
                g = jnp.where(first, grad, 0.0)
                sent.append(jnp.where(second, 0.0, g) + jnp.where(mask, 0.0, v))
                kept.append(jnp.where(second, g, 0.0) + jnp.where(mask, v, 0.0))
            outs[0][q, sl] = jnp.where(upper, sent[1], sent[0])
            outs[1][q, sl] = jnp.where(upper, sent[0], sent[1])
            outs[2][q, sl] = jnp.where(upper, kept[1], kept[0])
            outs[3][q, sl] = jnp.where(upper, kept[0], kept[1])


def presum_kernel(spot, *refs):
    for c in range(2):
        for q in range(2):
            for sl, _, _ in chunks():
                a, b, x = (refs[3 * c + i][q, sl] for i in range(3))
                refs[6 + c][q, sl] = (a + b) + x


def final_kernel(spot, *refs):
    out, buffer, done = refs[4], refs[5], refs[6]
    copies = []
    for q in range(2):
        for c in range(2):
            for sl, _, _ in chunks():
                buffer[q, c, sl] = refs[c][q, sl] + refs[2 + c][q, sl]
            copies.append(pltpu.make_async_copy(buffer.at[q, c], out.at[q, c], done.at[2 * q + c]))
            copies[-1].start()
    for copy in copies:
        copy.wait()


def moved(t, dx, dy):
    return ((t // GX + dy) % ROWS) * GX + (t % GX + dx) % GX


def pairs_of(*per_core):
    out = []
    for d, step in enumerate(per_core):
        if step is not None:
            out += [(d * TILES + t, d * TILES + moved(t, *step)) for t in range(TILES)]
    return out


GATHER = (pairs_of((-1, 0), (1, 0)), pairs_of((0, -1), (0, 1)))
SCATTER = (pairs_of((1, 0), (-1, 0)), pairs_of((0, 1), (0, -1)))
INFO = (pairs_of((1, 0), (1, 0)), pairs_of((0, 1), (0, 1)))
CROSSED = [[(a, (b + TILES) % (2 * TILES)) for a, b in way] for way in SCATTER]
DIAGONAL = pairs_of(None, (1, 1))
SWAP = [(d * TILES + t, (1 - d) * TILES + t) for d in range(2) for t in range(TILES)]


def permute(block, pairs):
    return lax.ppermute(block, ("depth", "tiles"), pairs)


def fourier():
    row = lax.broadcasted_iota(jnp.int32, (N, N), 0)
    col = lax.broadcasted_iota(jnp.int32, (N, N), 1)
    phase = (row * col % N).astype(F32) * (2.0 * math.pi / N)
    scale = 1.0 / math.sqrt(N)
    return jnp.stack([jnp.cos(phase) * scale, -jnp.sin(phase) * scale])


def step(transmission, illumination, fresnel_taps, intensity, offsets, counts):
    core = lax.axis_index("depth").astype(jnp.int32)
    mine = transmission[:, :, 0]
    other = permute(mine, SWAP)
    alive = (core < counts[0]).astype(jnp.int32)
    info = jnp.concatenate([jnp.where(core == 0, offsets[0, 0], offsets[0, 1]), core[None], alive[None]])
    left = permute(info, INFO[0])
    up = permute(info, INFO[1])
    upleft = permute(info, DIAGONAL)
    here = jnp.where(core == 0, info, upleft)
    at_y = jnp.where(core == 0, up, left)
    at_x = jnp.where(core == 0, left, up)
    own = call(order_kernel, [FIELD] * 4, info, [mine, other])
    near = [permute(own[p], GATHER[p % 2]) for p in range(4)]
    far = []
    for p in range(4):
        mixed, = call(functools.partial(blend_kernel, p % 2 == 1), [FIELD], (at_y, at_x)[p % 2], [own[p], near[p]])
        far.append(permute(mixed, GATHER[1 - p % 2]))
    second_slot = intensity[0, 1]
    shared = permute(second_slot, DIAGONAL)

    tabs = tables(here, tap_rows(fresnel_taps), fourier())
    patch0, patch1, wave0, wave1, wave2 = call(
        first_kernel, [FIELD] * 5, here, [*own[:2], *near[:2], *far[:2], illumination, *tabs], WORK
    )
    patch2, patch3, wave3, spectrum = call(
        second_kernel, [FIELD] * 4, here, [*own[2:], *near[2:], *far[2:], wave2, *tabs], WORK
    )
    grad_high, x_high, y_high, state = call(
        turn_up_kernel, [PAIR, FIELD, FIELD, STATE], here,
        [spectrum, intensity[0, 0], shared, wave2, wave3, patch2, patch3, *tabs], WORK
    )
    came_high = [permute(x_high, SCATTER[0]), permute(y_high, SCATTER[1])]
    grad_low, came_low = [None, None], [None, None]
    for k in (1, 0):
        outs = call(
            functools.partial(up_kernel, k), [FIELD, PLANE, PLANE] + [STATE] * k, here,
            [state, (wave0, wave1)[k], (patch0, patch1)[k], *tabs], WORK
        )
        grad_low[k] = outs[0]
        came_low[k] = [permute(outs[1], SCATTER[0]), permute(outs[2], SCATTER[1])]
        state = outs[3] if k else None
    parts, crosses = [], []
    for channel, there in ((0, at_x), (1, at_y)):
        straight, cross, stay, leaving = call(
            functools.partial(turn_kernel, channel), [FIELD] * 4, jnp.concatenate([here, there]),
            [*grad_low, grad_high, came_low[0][channel], came_low[1][channel], came_high[channel]]
        )
        way = 1 - channel
        parts += [stay, permute(leaving, SWAP), permute(straight, SCATTER[way])]
        crosses.append(permute(cross, CROSSED[way]))
    sums = call(presum_kernel, [FIELD] * 2, here, parts)
    scratch = [pltpu.VMEM((2, 2, N, N), F32), pltpu.SemaphoreType.DMA((4,))]
    out, = call(final_kernel, [PAIR], here, [*sums, *crosses], scratch, pl.BlockSpec(memory_space=pl.ANY))
    return out[:, :, None]


def solution(mesh):
    placed = (
        P("depth", None, "tiles", None, None),
        P(),
        P(),
        P("tiles", None, None, None),
        P("tiles", None, None),
        P("tiles"),
    )
    return jax.shard_map(
        step,
        mesh=mesh,
        in_specs=placed,
        out_specs=P("depth", None, "tiles", None, None),
        check_vma=False,
    )
```
